32 devices in a mesh: rep: 2 (over x), fsdp: 16 (over z, y, core).
Axes of the slice: x: 2, y: 2, z: 4, core: 2. Of those that a mesh axis runs over, the one named last changes fastest.
Arguments:
- tokens_in: bfloat16 [37632, 768], P(('rep', 'fsdp')), may hold values from -6 to 6
- token_image: int32 [37632], P(('rep', 'fsdp')), may hold values from 0 to 5, as said below
- joined_weight: bfloat16 [768, 5376], P('fsdp'), may hold values from -0.21875 to 0.21875
- heads_weight: bfloat16 [768, 768], P('fsdp'), may hold values from -1.75 to 1.75
- down_weight: bfloat16 [3072, 768], P('fsdp'), may hold values from -0.109375 to 0.109375
- norm_gain: bfloat16 [768], P('fsdp'), may hold values from 0.25 to 1.75
- query_gain: bfloat16 [64], P('fsdp'), may hold values from 0.25 to 1.75
- key_gain: bfloat16 [64], P('fsdp'), may hold values from 0.25 to 1.75
- hidden_bias: bfloat16 [3072], P('fsdp'), may hold values from -3 to 3
- output_bias: bfloat16 [768], P('fsdp'), may hold values from -3 to 3
- cotangent: bfloat16 [37632, 768], P(('rep', 'fsdp')), may hold values from -6 to 6
Outputs:
- block_out: bfloat16 [37632, 768], P(('rep', 'fsdp'))
- grad_tokens: bfloat16 [37632, 768], P(('rep', 'fsdp'))
- grad_joined: float32 [768, 5376], P('fsdp')
- grad_heads: float32 [768, 768], P('fsdp')
- grad_down: float32 [3072, 768], P('fsdp')
- grad_norm: float32 [768], P('fsdp')
- grad_query: float32 [64], P('fsdp')
- grad_key: float32 [64], P('fsdp')
- grad_hidden: float32 [3072], P('fsdp')
- grad_output: float32 [768], P('fsdp')
The draws below stay inside these ranges and needn't reach their ends.
Inputs may be any that keep to these rules, and one draw needn't show every extreme that they name: `token_image`: in each aligned block of 1176 tokens (the tokens of one device) either all tokens are 0 (one image), or token t of the block is t // 196 (6 images of 196 consecutive tokens). In every draw some block holds one image and some block holds 6.
All inputs are finite; a program needn't handle non-finite values.
Results may differ from the reference program's by a relative error of at most 0.013.
Values may be sent and summed in bfloat16 or wider, within the bound.
No kernel may reach another device: no remote copies, remote signals or barrier semaphores. Data moves between devices by JAX's collectives and lax.ppermute only.
A program may use at most 320 MiB of HBM per device.

```python
import jax
import jax.numpy as jnp
from jax import lax

D = 768
H = 12
HD = 64
FF = 3072
SHORT = 196
TOK_DEV = 1176
TOKENS = 37632
JOINED = 5376


def draw_token_image(key, part):
    devices = TOKENS // TOK_DEV
    key_flag, key_one, key_two = jax.random.split(key, 3)
    long_flag = (jax.random.randint(key_flag, (devices,), 0, 4) == 0).astype(jnp.int32)
    chosen_long = jax.random.randint(key_one, (), 0, devices)
    chosen_short = (chosen_long + 1 + jax.random.randint(key_two, (), 0, devices - 1)) % devices
    device_index = jnp.arange(devices)
    long_flag = jnp.where(device_index == chosen_long, 1, long_flag)
    long_flag = jnp.where(device_index == chosen_short, 0, long_flag)
    position = jnp.arange(TOK_DEV)
    local_image = jnp.where(long_flag[:, None] == 1, 0, position[None, :] // SHORT)
    return local_image.reshape(TOKENS).astype(jnp.int32)


def level_of(rng, extent, pieces, low, high):
    def one(dim, shards_of):
        draws = jax.random.uniform(jax.random.fold_in(jax.random.fold_in(rng, 6), dim), (shards_of,), jnp.float32, low / len(pieces), high / len(pieces))
        return jnp.repeat(jnp.exp(draws), extent[dim] // shards_of).reshape((-1,) + (1,) * (len(extent) - dim - 1))

    gain = one(*pieces[0])
    for cut in pieces[1:]:
        gain = gain * one(*cut)
    return gain


def scatter_about(stream_key, extent, width, limit, pieces=(), kind=jnp.bfloat16):
    values = width * jax.random.normal(stream_key, extent, jnp.float32)
    if pieces:
        values = values * level_of(stream_key, extent, pieces, -0.22, 0.18)
    return jnp.clip(values, -limit, limit).astype(kind)


def setup_inputs(seed: int = 0) -> dict:
    splits = jax.random.split(jax.random.key(seed), 12)
    tokens_in = scatter_about(splits[0], (TOKENS, D), 1.0, 6.0, ((0, 32),))
    token_image = draw_token_image(jax.random.fold_in(splits[11], 71), 0)
    joined_weight = scatter_about(splits[2], (D, JOINED), D ** -0.5, 0.21875, ((0, 16),))
    heads_weight = scatter_about(splits[3], (D, D), (D // 64) ** -0.5, 1.75, ((0, 16),))
    down_weight = scatter_about(splits[4], (FF, D), FF ** -0.5, 0.109375, ((0, 16),))
    norm_gain = jnp.clip(1.0 + 0.15 * jax.random.normal(splits[5], (D,), jnp.float32), 0.25, 1.75).astype(jnp.bfloat16)
    query_gain = jnp.clip(1.0 + 0.15 * jax.random.normal(splits[6], (HD,), jnp.float32), 0.25, 1.75).astype(jnp.bfloat16)
    key_gain = jnp.clip(1.0 + 0.15 * jax.random.normal(splits[7], (HD,), jnp.float32), 0.25, 1.75).astype(jnp.bfloat16)
    hidden_bias = scatter_about(splits[8], (FF,), 0.5, 3.0, ((0, 16),))
    output_bias = scatter_about(splits[9], (D,), 0.5, 3.0, ((0, 16),))
    cotangent = scatter_about(splits[10], (TOKENS, D), 1.0, 6.0, ((0, 32),))
    return dict(tokens_in=tokens_in, token_image=token_image, joined_weight=joined_weight, heads_weight=heads_weight, down_weight=down_weight, norm_gain=norm_gain, query_gain=query_gain, key_gain=key_gain, hidden_bias=hidden_bias, output_bias=output_bias, cotangent=cotangent)


norm_eps = 1e-06

@jax.custom_vjp
def low(v):
    return lax.optimization_barrier(v.astype(jnp.bfloat16)).astype(jnp.float32)

@jax.custom_vjp
def low_back(v):
    return v

def low_keep(v):
    return (low(v), None)

def low_pass(kept, grad):
    return (grad,)

def back_keep(v):
    return (v, None)

def back_low(kept, grad):
    return (low(grad),)
low.defvjp(low_keep, low_pass)
low_back.defvjp(back_keep, back_low)

def layer_norm(values, gain_row):
    row_mean = lax.optimization_barrier(jnp.mean(values, axis=-1, keepdims=True))
    centered = values - row_mean
    variance = lax.optimization_barrier(jnp.mean(centered * centered, axis=-1, keepdims=True))
    return centered * lax.rsqrt(variance + norm_eps) * gain_row

def block_rows(params, token_rows, image_rows):
    joined_matrix, heads_matrix, down_matrix, gain_norm, gain_query, gain_key, bias_hidden, bias_output = params
    length = token_rows.shape[0]
    highest = lax.Precision.HIGHEST
    normed = low(layer_norm(token_rows, gain_norm))
    hidden = low_back(jnp.dot(normed, joined_matrix, precision=highest))
    queries = low(layer_norm(hidden[:, :D].reshape(length, H, HD), gain_query))
    keys_normed = low(layer_norm(hidden[:, D:2 * D].reshape(length, H, HD), gain_key))
    values = low(hidden[:, 2 * D:3 * D]).reshape(length, H, HD)
    scores = low_back(jnp.einsum('qhd,khd->hqk', queries, keys_normed, precision=highest) * HD ** (-0.5))
    same_image = image_rows[:, None] == image_rows[None, :]
    scores = jnp.where(same_image[None], scores, -1e+30)
    probs = jax.nn.softmax(scores, axis=-1)
    mixed = jnp.einsum('hqk,khd->qhd', low(probs), values, precision=highest).reshape(length, D)
    mixed = low_back(low(mixed))
    activated = low(jax.nn.gelu(hidden[:, 3 * D:] + bias_hidden, approximate=False))
    attended = jnp.dot(mixed, heads_matrix, precision=highest)
    branch_mlp = jnp.dot(activated, down_matrix, precision=highest) + bias_output
    return token_rows + attended + branch_mlp

def reference(tokens_in, token_image, joined_weight, heads_weight, down_weight, norm_gain, query_gain, key_gain, hidden_bias, output_bias, cotangent):
    params = tuple((array_in.astype(jnp.float32) for array_in in (joined_weight, heads_weight, down_weight, norm_gain, query_gain, key_gain, hidden_bias, output_bias)))
    token_rows = tokens_in.astype(jnp.float32)
    image_blocks = token_image.reshape(-1, TOK_DEV).astype(jnp.int32)
    step_block = jax.checkpoint(block_rows)

    def forward(rows_all, weights_all):

        def scan_step(carry_unused, inputs_block):
            return (carry_unused, step_block(weights_all, inputs_block[0], inputs_block[1]))
        _, outputs = lax.scan(scan_step, jnp.zeros((), jnp.float32), (rows_all.reshape(-1, TOK_DEV, D), image_blocks))
        return outputs.reshape(-1, D)
    block_sum, backward = jax.vjp(forward, token_rows, params)
    grad_rows, grad_params = backward(cotangent.astype(jnp.float32))
    return (block_sum.astype(jnp.bfloat16), grad_rows.astype(jnp.bfloat16), grad_params[0], grad_params[1], grad_params[2], grad_params[3], grad_params[4], grad_params[5], grad_params[6], grad_params[7])
```

```python
import functools

import jax
import jax.numpy as jnp
from jax import lax
from jax.experimental import pallas as pl
from jax.experimental.pallas import tpu as pltpu
from jax.sharding import PartitionSpec as P

F32 = jnp.float32
BF = jnp.bfloat16
EPS = 1e-06
GROUPS = 16
SMALL = 16
HEAD = 64
PAIR = 128
CHUNK = 256
FAR = -512.0
VMEM_LIMIT = 62 << 20


def dg(left, right, left_dim, right_dim):
    return lax.dot_general(
        left, right, (((left_dim,), (right_dim,)), ((), ())), preferred_element_type=F32
    )


def spans(total, step):
    return [(start, min(step, total - start)) for start in range(0, total, step)]


def split_low(values):
    high = values.astype(BF)
    return high, (values - high.astype(F32)).astype(BF)


def block_ones(size, scale, flip=0):
    row = lax.broadcasted_iota(jnp.int32, (size, size), 0) // HEAD
    col = lax.broadcasted_iota(jnp.int32, (size, size), 1) // HEAD
    return jnp.where(row == (col ^ flip), scale, 0.0).astype(BF)


def head_sum(values, ones):
    high, low = split_low(values)
    return dg(high, ones, 1, 0) + dg(low, ones, 1, 0)


def row_norm(rows):
    mean = jnp.mean(rows, axis=-1, keepdims=True)
    centered = rows - mean
    variance = jnp.mean(centered * centered, axis=-1, keepdims=True)
    inverse = lax.rsqrt(variance + EPS)
    return centered * inverse, inverse


def small_rows(small_ref):
    return jnp.sum(small_ref[...].astype(F32), axis=0)


def square(block_ref):
    groups, rows, width = block_ref.shape
    return block_ref[...].reshape(groups * rows, width)


def params(steps):
    return pltpu.CompilerParams(
        dimension_semantics=("arbitrary",) * steps, vmem_limit_bytes=VMEM_LIMIT
    )


def cost(flops, moved, special=0):
    return pl.CostEstimate(flops=int(flops), bytes_accessed=int(moved), transcendentals=int(special))


def project_kernel(token_ref, weight_ref, small_ref, low_ref, hat_ref, inv_ref, normed_ref, pre_ref):
    section = pl.program_id(0)
    rows = small_rows(small_ref)

    @pl.when(section == 0)
    def _():
        for start, size in spans(token_ref.shape[0], CHUNK):
            hat, _ = row_norm(token_ref[start : start + size, :].astype(F32))
            normed_ref[start : start + size, :] = (hat * rows[0:1, :]).astype(BF)

    weight = square(weight_ref)

    @pl.when(section < 2)
    def _():
        ones = block_ones(2 * PAIR, 1.0 / HEAD)
        gain_pair = jnp.where(section == 0, rows[6:7, :PAIR], rows[6:7, PAIR : 2 * PAIR])
        gain = jnp.concatenate([gain_pair, gain_pair], axis=1)
        factor = jnp.where(section == 0, HEAD**-0.5, 1.0).astype(F32)
        for start, size in spans(token_ref.shape[0], CHUNK):
            part = slice(start, start + size)
            pre_ref[:size, :] = dg(normed_ref[part, :], weight, 1, 0)
            for left, wide in spans(pre_ref.shape[1], 2 * PAIR):
                lanes = slice(left, left + wide)
                pre = pre_ref[:size, lanes]
                centered = pre - head_sum(pre, ones)
                inverse = lax.rsqrt(head_sum(centered * centered, ones) + EPS)
                hat = centered * inverse
                hat_ref[0, part, lanes] = hat
                inv_ref[0, part, lanes] = inverse
                low_ref[0, part, lanes] = ((hat * gain).astype(BF).astype(F32) * factor).astype(BF)

    @pl.when(section == 2)
    def _():
        for start, size in spans(token_ref.shape[0], CHUNK):
            part = slice(start, start + size)
            low_ref[0, part, :] = dg(normed_ref[part, :], weight, 1, 0).astype(BF)


def project(tokens, gathered):
    length, width = tokens.shape
    rows = width // GROUPS
    full = pl.BlockSpec((length, width), lambda s: (0, 0))
    return pl.pallas_call(
        project_kernel,
        grid=(3,),
        in_specs=[
            full,
            pl.BlockSpec((GROUPS, rows, width), lambda s: (0, s, 0)),
            pl.BlockSpec((GROUPS, SMALL, width), lambda s: (0, 4 * rows // SMALL, 0)),
        ],
        out_specs=[
            pl.BlockSpec((1, length, width), lambda s: (s, 0, 0)),
            pl.BlockSpec((1, length, width), lambda s: (jnp.minimum(s, 1), 0, 0)),
            pl.BlockSpec((1, length, width), lambda s: (jnp.minimum(s, 1), 0, 0)),
            full,
        ],
        out_shape=[
            jax.ShapeDtypeStruct((3, length, width), BF),
            jax.ShapeDtypeStruct((2, length, width), F32),
            jax.ShapeDtypeStruct((2, length, width), F32),
            jax.ShapeDtypeStruct((length, width), BF),
        ],
        scratch_shapes=[pltpu.VMEM((CHUNK, width), F32)],
        compiler_params=params(1),
        cost_estimate=cost(9 * length * width * width, 40 * length * width),
        name="project",
    )(tokens, gathered, gathered)


def own_lanes(length, head):
    lane = lax.broadcasted_iota(jnp.int32, (length, PAIR), 1)
    return (lane // HEAD) == head


def attend_kernel(query_ref, key_ref, value_ref, near_ref, far_ref, exps_ref, mixed_ref, wide_ref, inv_ref):
    length = query_ref.shape[1]
    values = jnp.concatenate([value_ref[0], jnp.ones((length, PAIR), BF)], axis=1)
    for head in range(2):
        own = own_lanes(length, head)
        keys = jnp.where(own, key_ref[0], far_ref[...])
        for start, size in spans(length, CHUNK):
            part = slice(start, start + size)
            own_part = own_lanes(size, head)
            queries = jnp.where(own_part, query_ref[0, part, :], near_ref[part, :])
            exps = jnp.exp(dg(queries, keys, 1, 1)).astype(BF)
            exps_ref[head, part, :] = exps
            both = dg(exps, values, 1, 0)
            inverse = 1.0 / both[:, PAIR:]
            out = both[:, :PAIR] * inverse
            if head == 1:
                out = jnp.where(own_part, out, wide_ref[part, :])
                inverse = jnp.where(own_part, inverse, inv_ref[part, :])
                mixed_ref[part, :] = out.astype(BF)
            wide_ref[part, :] = out
            inv_ref[part, :] = inverse


def attend(low, near, far):
    _, length, width = low.shape
    pairs = width // PAIR
    lanes = pl.BlockSpec((length, PAIR), lambda p: (0, p))
    fixed = pl.BlockSpec((length, PAIR), lambda p: (0, 0))
    return pl.pallas_call(
        attend_kernel,
        grid=(pairs,),
        in_specs=[pl.BlockSpec((1, length, PAIR), lambda p, k=k: (k, 0, p)) for k in range(3)]
        + [fixed, fixed],
        out_specs=[pl.BlockSpec((2, length, length), lambda p: (p, 0, 0)), lanes, lanes, lanes],
        out_shape=[
            jax.ShapeDtypeStruct((2 * pairs, length, length), BF),
            jax.ShapeDtypeStruct((length, width), BF),
            jax.ShapeDtypeStruct((length, width), F32),
            jax.ShapeDtypeStruct((length, width), F32),
        ],
        compiler_params=params(1),
        cost_estimate=cost(pairs * 2 * 8 * PAIR * length * length, 24 * length * length),
        name="attend",
    )(low, low, low, near, far)


def mlp_kernel(
    normed_ref,
    cot_ref,
    up_ref,
    down_ref,
    small_ref,
    branch_ref,
    back_ref,
    hidden_ref,
    grads_ref,
    small_s,
    act_s,
    grad_s,
    up_s,
    down_s,
    sems,
):
    step = pl.program_id(0)
    length, width = normed_ref.shape
    rows = width // GROUPS
    small_s[...] = small_rows(small_ref)
    bias = small_s[pl.ds(2 + step, 1), :]
    up = square(up_ref)
    down = square(down_ref)
    hidden = jnp.zeros((1, width), F32)
    for start, size in spans(length, CHUNK):
        part = slice(start, start + size)
        inner = dg(normed_ref[part, :], up, 1, 0) + bias
        cdf = 0.5 + 0.5 * lax.erf(inner * (0.5**0.5))
        pdf = jnp.exp(inner * inner * -0.5) * 0.3989422804014327
        act = (inner * cdf).astype(BF)
        grad = dg(cot_ref[part, :], down, 1, 1) * (cdf + inner * pdf)
        hidden = hidden + jnp.sum(grad, axis=0, keepdims=True)
        grad_low = grad.astype(BF)
        act_s[part, :] = act
        grad_s[part, :] = grad_low
        forward = dg(act, down, 1, 0)
        backward = dg(grad_low, up, 1, 1)

        @pl.when(step == 0)
        def _():
            branch_ref[part, :] = forward
            back_ref[part, :] = backward

        @pl.when(step > 0)
        def _():
            branch_ref[part, :] = branch_ref[part, :] + forward
            back_ref[part, :] = back_ref[part, :] + backward

    hidden_ref[0] = hidden
    groups = GROUPS // pl.num_programs(0)

    def copies(index):
        return (
            pltpu.make_async_copy(
                up_s, grads_ref.at[:, pl.ds(pl.multiple_of(index * rows, rows), rows), :], sems.at[0]
            ),
            pltpu.make_async_copy(
                down_s,
                grads_ref.at[pl.ds(index * groups, groups), pl.ds(4 * rows, 4 * rows), :],
                sems.at[1],
            ),
        )

    @pl.when(step > 0)
    def _():
        for copy in copies(step - 1):
            copy.wait()

    up_s[...] = dg(normed_ref[...], grad_s[...], 0, 0).astype(BF).reshape(up_s.shape)
    down_s[...] = dg(act_s[...], cot_ref[...], 0, 0).astype(BF).reshape(down_s.shape)
    for copy in copies(step):
        copy.start()

    @pl.when(step == pl.num_programs(0) - 1)
    def _():
        for copy in copies(step):
            copy.wait()


def mlp(normed, cotangent, gathered, gathered_small):
    length, width = normed.shape
    rows = width // GROUPS
    steps = 4
    full = pl.BlockSpec((length, width), lambda s: (0, 0))
    return pl.pallas_call(
        mlp_kernel,
        grid=(steps,),
        in_specs=[
            full,
            full,
            pl.BlockSpec((GROUPS, rows, width), lambda s: (0, s, 0)),
            pl.BlockSpec((GROUPS // steps, steps * rows, width), lambda s: (s, 1, 0)),
            pl.BlockSpec((GROUPS, SMALL, width), lambda s: (0, 4 * rows // SMALL, 0)),
        ],
        out_specs=[
            full,
            full,
            pl.BlockSpec((1, 1, width), lambda s: (s, 0, 0)),
            pl.BlockSpec(memory_space=pl.ANY),
        ],
        out_shape=[
            jax.ShapeDtypeStruct((length, width), F32),
            jax.ShapeDtypeStruct((length, width), F32),
            jax.ShapeDtypeStruct((steps, 1, width), F32),
            jax.ShapeDtypeStruct((GROUPS, 8 * rows, width), BF),
        ],
        scratch_shapes=[
            pltpu.VMEM((SMALL, width), F32),
            pltpu.VMEM((length, width), BF),
            pltpu.VMEM((length, width), BF),
            pltpu.VMEM((GROUPS, rows, width), BF),
            pltpu.VMEM((GROUPS // steps, steps * rows, width), BF),
            pltpu.SemaphoreType.DMA((2,)),
        ],
        compiler_params=params(1),
        cost_estimate=cost(48 * length * width * width, 40 * length * width, 8 * length * width),
        name="mlp",
    )(normed, cotangent, gathered, gathered, gathered_small)


def backward_kernel(
    query_ref,
    key_ref,
    value_ref,
    exps_ref,
    wide_ref,
    inv_ref,
    cot_ref,
    heads_ref,
    small_ref,
    qhat_ref,
    khat_ref,
    qinv_ref,
    kinv_ref,
    grad_ref,
    sums_ref,
    heads_s,
    dot_s,
    delta_s,
    query_s,
    key_s,
    value_s,
):
    pair = pl.program_id(0)
    length = query_ref.shape[1]

    @pl.when(pair == 0)
    def _():
        heads_s[...] = square(heads_ref)
        sums_ref[...] = jnp.zeros_like(sums_ref)

    rows = small_rows(small_ref)
    flipped = block_ones(PAIR, 1.0, 1)
    head_rows = heads_s[pl.ds(pl.multiple_of(pair * PAIR, PAIR), PAIR), :]
    for start, size in spans(length, CHUNK):
        part = slice(start, start + size)
        grad = dg(cot_ref[part, :], head_rows, 1, 1) * inv_ref[part, :]
        low = grad.astype(BF)
        dot_s[part, :] = low
        delta_s[part, :] = head_sum(low.astype(F32) * wide_ref[part, :], flipped)

    for head in range(2):
        lane = lax.broadcasted_iota(jnp.int32, (length, PAIR), 1)
        own = (lane // HEAD) == head
        values = jnp.where(own, value_ref[0], jnp.where(lane % HEAD < 2, 1.0, 0.0).astype(BF))
        for start, size in spans(length, CHUNK):
            part = slice(start, start + size)
            lane_p = lax.broadcasted_iota(jnp.int32, (size, PAIR), 1)
            own_p = (lane_p // HEAD) == head
            high, rest = split_low(-delta_s[part, :])
            extra = jnp.where(
                lane_p % HEAD == 0, high, jnp.where(lane_p % HEAD == 1, rest, jnp.zeros_like(rest))
            )
            dots = dot_s[part, :]
            slopes = dg(jnp.where(own_p, dots, extra), values, 1, 1)
            exps = exps_ref[head, part, :]
            scores = (exps.astype(F32) * slopes).astype(BF)
            dq = dg(scores, key_ref[0], 1, 0)
            dk = dg(scores, query_ref[0, part, :], 0, 0)
            dv = dg(exps, dots, 0, 0)
            if head == 1:
                dq = jnp.where(own_p, dq, query_s[part, :])
            query_s[part, :] = dq
            if start == 0:
                key_s[head] = dk
                value_s[head] = dv
            else:
                key_s[head] = key_s[head] + dk
                value_s[head] = value_s[head] + dv

    ones = block_ones(PAIR, 1.0 / HEAD)
    for start, size in spans(length, CHUNK):
        part = slice(start, start + size)
        own_p = own_lanes(size, 0)
        both = (
            (query_s[part, :] * HEAD**-0.5, qhat_ref, qinv_ref, rows[6:7, :PAIR]),
            (
                jnp.where(own_p, key_s[0, part, :], key_s[1, part, :]),
                khat_ref,
                kinv_ref,
                rows[6:7, PAIR : 2 * PAIR],
            ),
        )
        for index, (grad, hat_ref, inverse_ref, gain) in enumerate(both):
            hat = hat_ref[0, part, :]
            product = grad * hat
            sums_ref[index : index + 1, :] += jnp.sum(product, axis=0, keepdims=True)
            mean = head_sum(grad * gain, ones)
            along = head_sum(product * gain, ones)
            grad_ref[index, part, :] = (
                inverse_ref[0, part, :] * (grad * gain - mean - hat * along)
            ).astype(BF)
        grad_ref[2, part, :] = jnp.where(own_p, value_s[0, part, :], value_s[1, part, :]).astype(BF)


def attend_back(low, exps, wide, inverse, cotangent, gathered, hat, inv):
    _, length, width = low.shape
    rows = width // GROUPS
    pairs = width // PAIR
    lanes = pl.BlockSpec((length, PAIR), lambda p: (0, p))

    def third(k):
        return pl.BlockSpec((1, length, PAIR), lambda p: (k, 0, p))

    return pl.pallas_call(
        backward_kernel,
        grid=(pairs,),
        in_specs=[third(k) for k in range(3)]
        + [
            pl.BlockSpec((2, length, length), lambda p: (p, 0, 0)),
            lanes,
            lanes,
            pl.BlockSpec((length, width), lambda p: (0, 0)),
            pl.BlockSpec((GROUPS, rows, width), lambda p: (0, 3, 0)),
            pl.BlockSpec((GROUPS, SMALL, width), lambda p: (0, 4 * rows // SMALL, 0)),
            third(0),
            third(1),
            third(0),
            third(1),
        ],
        out_specs=[
            pl.BlockSpec((3, length, PAIR), lambda p: (0, 0, p)),
            pl.BlockSpec((8, PAIR), lambda p: (0, 0)),
        ],
        out_shape=[
            jax.ShapeDtypeStruct((3, length, width), BF),
            jax.ShapeDtypeStruct((8, PAIR), F32),
        ],
        scratch_shapes=[
            pltpu.VMEM((width, width), BF),
            pltpu.VMEM((length, PAIR), BF),
            pltpu.VMEM((length, PAIR), F32),
            pltpu.VMEM((length, PAIR), F32),
            pltpu.VMEM((2, length, PAIR), F32),
            pltpu.VMEM((2, length, PAIR), F32),
        ],
        compiler_params=params(1),
        cost_estimate=cost(pairs * 2 * 16 * PAIR * length * length, 24 * length * length),
        name="attend_back",
    )(low, low, low, exps, wide, inverse, cotangent, gathered, gathered, hat, hat, inv, inv)


def weights_kernel(normed_ref, grad_ref, mixed_ref, cot_ref, out_ref):
    section = pl.program_id(0)

    @pl.when(section < 3)
    def _():
        out_ref[...] = dg(normed_ref[...], grad_ref[0], 0, 0).astype(BF).reshape(out_ref.shape)

    @pl.when(section == 3)
    def _():
        out_ref[...] = dg(mixed_ref[...], cot_ref[...], 0, 0).astype(BF).reshape(out_ref.shape)


def weight_grads(normed, grads, mixed, cotangent):
    _, length, width = grads.shape
    rows = width // GROUPS
    full = pl.BlockSpec((length, width), lambda s: (0, 0))
    return pl.pallas_call(
        weights_kernel,
        grid=(4,),
        in_specs=[
            full,
            pl.BlockSpec((1, length, width), lambda s: (jnp.minimum(s, 2), 0, 0)),
            full,
            full,
        ],
        out_specs=pl.BlockSpec((GROUPS, rows, width), lambda s: (0, s, 0)),
        out_shape=jax.ShapeDtypeStruct((GROUPS, 4 * rows, width), BF),
        compiler_params=params(1),
        cost_estimate=cost(8 * length * width * width, 14 * length * width),
        name="weight_grads",
    )(normed, grads, mixed, cotangent)


def tail_kernel(
    grad_ref,
    weight_ref,
    small_ref,
    token_ref,
    cot_ref,
    mixed_ref,
    branch_ref,
    back_ref,
    out_ref,
    token_grad_ref,
    total_s,
):
    section = pl.program_id(0)
    length = token_ref.shape[0]
    weight = square(weight_ref)

    @pl.when(section == 0)
    def _():
        for start, size in spans(length, CHUNK):
            part = slice(start, start + size)
            total_s[part, :] = back_ref[part, :] + dg(grad_ref[0, part, :], weight, 1, 1)

    @pl.when((section > 0) & (section < 3))
    def _():
        for start, size in spans(length, CHUNK):
            part = slice(start, start + size)
            total_s[part, :] = total_s[part, :] + dg(grad_ref[0, part, :], weight, 1, 1)

    @pl.when(section == 3)
    def _():
        rows = small_rows(small_ref)
        for start, size in spans(length, CHUNK):
            part = slice(start, start + size)
            tokens = token_ref[part, :].astype(F32)
            attended = dg(mixed_ref[part, :], weight, 1, 0)
            out_ref[part, :] = (tokens + attended + branch_ref[part, :] + rows[1:2, :]).astype(BF)
            hat, inverse = row_norm(tokens)
            grad = total_s[part, :] * rows[0:1, :]
            mean = jnp.mean(grad, axis=-1, keepdims=True)
            along = jnp.mean(grad * hat, axis=-1, keepdims=True)
            token_grad_ref[part, :] = (
                cot_ref[part, :].astype(F32) + inverse * (grad - mean - hat * along)
            ).astype(BF)


def tail(grads, gathered, tokens, cotangent, mixed, branch, back):
    _, length, width = grads.shape
    rows = width // GROUPS
    full = pl.BlockSpec((length, width), lambda s: (0, 0))
    return pl.pallas_call(
        tail_kernel,
        grid=(4,),
        in_specs=[
            pl.BlockSpec((1, length, width), lambda s: (jnp.minimum(s, 2), 0, 0)),
            pl.BlockSpec((GROUPS, rows, width), lambda s: (0, s, 0)),
            pl.BlockSpec((GROUPS, SMALL, width), lambda s: (0, 4 * rows // SMALL, 0)),
            full,
            full,
            full,
            full,
            full,
        ],
        out_specs=[full, full],
        out_shape=[
            jax.ShapeDtypeStruct((length, width), BF),
            jax.ShapeDtypeStruct((length, width), BF),
        ],
        scratch_shapes=[pltpu.VMEM((length, width), F32)],
        compiler_params=params(1),
        cost_estimate=cost(8 * length * width * width, 24 * length * width),
        name="tail",
    )(grads, gathered, gathered, tokens, cotangent, mixed, branch, back)


def place(vector, offset, total):
    return lax.dynamic_update_slice(jnp.zeros((total,), vector.dtype), vector, (offset,))


def stack_columns(shard, first, count, width):
    return [shard[:, (first + k) * width : (first + k + 1) * width] for k in range(count)]


def regroup(gathered, section_rows):
    devices, _, width = gathered.shape
    if devices == GROUPS:
        return gathered
    fold = devices // GROUPS
    parts, start = [], 0
    for rows, small in section_rows:
        piece = gathered[:, start : start + rows, :]
        start += rows
        if small:
            parts.append(piece.reshape(GROUPS, fold, rows, width).sum(1))
        else:
            parts.append(piece.reshape(GROUPS, fold * rows, width))
    return jnp.concatenate(parts, axis=1)


def ungroup(grouped, section_rows, devices):
    if devices == GROUPS:
        return grouped
    fold = devices // GROUPS
    width = grouped.shape[2]
    parts, start = [], 0
    for rows, small in section_rows:
        wide = rows if small else rows * fold
        piece = grouped[:, start : start + wide, :]
        start += wide
        if small:
            parts.append(jnp.repeat(piece, fold, axis=0))
        else:
            parts.append(piece.reshape(devices, rows, width))
    return jnp.concatenate(parts, axis=1)


def per_device(
    devices,
    tokens_in,
    token_image,
    joined_weight,
    heads_weight,
    down_weight,
    norm_gain,
    query_gain,
    key_gain,
    hidden_bias,
    output_bias,
    cotangent,
):
    length, width = tokens_in.shape
    rows = joined_weight.shape[0]
    me = lax.axis_index("fsdp")
    thin, bias_thin, head_thin = norm_gain.shape[0], hidden_bias.shape[0], query_gain.shape[0]

    small = (
        place(norm_gain, me * thin, SMALL * width)
        + place(output_bias, width + me * thin, SMALL * width)
        + place(hidden_bias, 2 * width + me * bias_thin, SMALL * width)
    )
    for index, vector in enumerate((query_gain, query_gain, key_gain, key_gain)):
        small = small + place(vector, 6 * width + index * HEAD + me * head_thin, SMALL * width)
    first_rows = [(rows, False)] * 4 + [(SMALL, True)]
    first = jnp.concatenate(
        stack_columns(joined_weight, 0, 3, width) + [heads_weight, small.reshape(SMALL, width)], axis=0
    )
    gathered = regroup(lax.all_gather(first, "fsdp", axis=0), first_rows)

    second_rows = [(rows, False)] * 4 + [(4 * rows, False)]
    second = jnp.concatenate(stack_columns(joined_weight, 3, 4, width) + [down_weight], axis=0)
    second, _ = lax.optimization_barrier((second, gathered[0, 0, 0]))
    gathered_mlp = regroup(lax.all_gather(second, "fsdp", axis=0), second_rows)

    lane = lax.broadcasted_iota(jnp.int32, (length, PAIR), 1) % HEAD
    same = lane == token_image[:, None]
    near = jnp.where(same, 1.0, 0.0).astype(BF)
    far = jnp.where(same | (lane >= 6), 0.0, FAR).astype(BF)

    low, hat, inv, normed = project(tokens_in, gathered)
    exps, mixed, wide, inverse = attend(low, near, far)
    branch, back, hidden, mlp_grads = mlp(normed, cotangent, gathered_mlp, gathered)

    owner = lax.broadcasted_iota(jnp.int32, (GROUPS, 1, width), 0)
    at = lax.broadcasted_iota(jnp.int32, (GROUPS, 1, width), 2)
    per_group = width // GROUPS
    grad_output = jnp.sum(cotangent.astype(F32), axis=0)[None, None, :]
    vectors = [jnp.where(at // per_group == owner, grad_output, 0.0)]
    for k in range(4):
        block = at // (4 * per_group) + k * (GROUPS // 4)
        vectors.append(jnp.where(block == owner, hidden[k][None], 0.0))
    vectors.append(jnp.zeros((GROUPS, SMALL - 5, width), F32))
    early_small = jnp.concatenate(vectors, axis=1).astype(BF)

    grads, sums = attend_back(low, exps, wide, inverse, cotangent, gathered, hat, inv)
    late_grads = weight_grads(normed, grads, mixed, cotangent)
    query_sum = sums[0, :HEAD] + sums[0, HEAD:]
    key_sum = sums[1, :HEAD] + sums[1, HEAD:]
    packed = jnp.pad(jnp.concatenate([query_sum, key_sum]), (0, width - 2 * HEAD))[None, None, :]
    late_small = jnp.where((at % HEAD) // (HEAD // GROUPS) == owner, packed, 0.0)
    late_small = jnp.pad(late_small, ((0, 0), (0, SMALL - 1), (0, 0))).astype(BF)
    block_out, grad_tokens = tail(grads, gathered, tokens_in, cotangent, mixed, branch, back)

    def reduce(array, section_rows):
        array = ungroup(array, section_rows, devices)
        return lax.psum_scatter(array, "fsdp", scatter_dimension=0, tiled=True)[0]

    def both(array):
        return lax.psum(array, "rep").astype(F32)

    mlp_total = both(reduce(mlp_grads, second_rows))
    late_total = both(reduce(late_grads, first_rows[:4]))
    small_total = both(
        reduce(jnp.concatenate([early_small, late_small], axis=1), [(2 * SMALL, True)])
    )

    total_joined = jnp.concatenate(
        [late_total[k * rows : (k + 1) * rows] for k in range(3)]
        + [mlp_total[k * rows : (k + 1) * rows] for k in range(4)],
        axis=1,
    )
    total_heads = late_total[3 * rows : 4 * rows]
    total_down = mlp_total[4 * rows :]
    total_norm = jnp.sum(joined_weight.astype(F32) * total_joined, axis=1) / norm_gain.astype(F32)

    def take(row, offset, size):
        return lax.dynamic_slice(small_total, (row, offset), (1, size))[0]

    flat = me * bias_thin
    total_output = take(0, me * thin, thin)
    total_hidden = take(1 + flat // width, flat % width, bias_thin)
    total_query = take(SMALL, me * head_thin, head_thin)
    total_key = take(SMALL, HEAD + me * head_thin, head_thin)
    return (
        block_out,
        grad_tokens,
        total_joined,
        total_heads,
        total_down,
        total_norm,
        total_query,
        total_key,
        total_hidden,
        total_output,
    )


def solution(mesh):
    tokens, shard, thin = P(("rep", "fsdp"), None), P("fsdp", None), P("fsdp")
    return jax.shard_map(
        functools.partial(per_device, mesh.shape["fsdp"]),
        mesh=mesh,
        in_specs=(tokens, P(("rep", "fsdp")), shard, shard, shard, thin, thin, thin, thin, thin, tokens),
        out_specs=(tokens, tokens, shard, shard, shard, thin, thin, thin, thin, thin),
        check_vma=False,
    )
```

```python
import functools

import jax
import jax.numpy as jnp
from jax import lax
from jax.experimental import pallas as pl
from jax.experimental.pallas import tpu as pltpu
from jax.sharding import PartitionSpec as P

F32 = jnp.float32
BF = jnp.bfloat16
EPS = 1e-06
GROUPS = 16
SMALL = 16
HEAD = 64
PAIR = 128
CHUNK = 256
FAR = -512.0
VMEM_LIMIT = 62 << 20


def dg(left, right, left_dim, right_dim):
    return lax.dot_general(
        left, right, (((left_dim,), (right_dim,)), ((), ())), preferred_element_type=F32
    )


def spans(total, step):
    return [(start, min(step, total - start)) for start in range(0, total, step)]


def split_low(values):
    high = values.astype(BF)
    return high, (values - high.astype(F32)).astype(BF)


def block_ones(size, scale, flip=0):
    row = lax.broadcasted_iota(jnp.int32, (size, size), 0) // HEAD
    col = lax.broadcasted_iota(jnp.int32, (size, size), 1) // HEAD
    return jnp.where(row == (col ^ flip), scale, 0.0).astype(BF)


def head_sum(values, ones):
    high, low = split_low(values)
    return dg(high, ones, 1, 0) + dg(low, ones, 1, 0)


def row_norm(rows):
    mean = jnp.mean(rows, axis=-1, keepdims=True)
    centered = rows - mean
    variance = jnp.mean(centered * centered, axis=-1, keepdims=True)
    inverse = lax.rsqrt(variance + EPS)
    return centered * inverse, inverse


def small_rows(small_ref):
    return jnp.sum(small_ref[...].astype(F32), axis=0)


def square(block_ref):
    groups, rows, width = block_ref.shape
    return block_ref[...].reshape(groups * rows, width)


def params(steps):
    return pltpu.CompilerParams(
        dimension_semantics=("arbitrary",) * steps, vmem_limit_bytes=VMEM_LIMIT
    )


def cost(flops, moved, special=0):
    return pl.CostEstimate(flops=int(flops), bytes_accessed=int(moved), transcendentals=int(special))


def source_of(me, core_flip, y_flip, z_back):
    z, y, core = me // 4, (me // 2) % 2, me % 2
    z, y, core = (z + 4 - z_back) % 4, (y + y_flip) % 2, (core + core_flip) % 2
    return (z * 2 + y) * 2 + core


ROUTES = [(c, y, k) for c in range(2) for y in range(2) for k in range(4)]


def project_kernel(me_ref, token_ref, *refs):
    pieces = refs[:GROUPS]
    low_ref, hat_ref, inv_ref, normed_ref, all_ref, pre_ref, sems = refs[GROUPS:]
    section = pl.program_id(0)
    width = token_ref.shape[1]
    group = width // GROUPS
    copies = [
        pltpu.make_async_copy(piece, all_ref.at[source_of(me_ref[0], *route)], sems.at[index])
        for index, (piece, route) in enumerate(zip(pieces, ROUTES))
    ]

    @pl.when(section == 0)
    def _():
        for copy in copies:
            copy.start()
        for copy in copies:
            copy.wait()

    rows = jnp.sum(all_ref[:, 4 * group :, :].astype(F32), axis=0)

    @pl.when(section == 0)
    def _():
        for start, size in spans(token_ref.shape[0], CHUNK):
            hat, _ = row_norm(token_ref[start : start + size, :].astype(F32))
            normed_ref[start : start + size, :] = (hat * rows[0:1, :]).astype(BF)

    weight = all_ref[:, pl.ds(pl.multiple_of(section * group, group), group), :].reshape(width, width)

    @pl.when(section < 2)
    def _():
        ones = block_ones(2 * PAIR, 1.0 / HEAD)
        gain_pair = jnp.where(section == 0, rows[6:7, :PAIR], rows[6:7, PAIR : 2 * PAIR])
        gain = jnp.concatenate([gain_pair, gain_pair], axis=1)
        factor = jnp.where(section == 0, HEAD**-0.5, 1.0).astype(F32)
        for start, size in spans(token_ref.shape[0], CHUNK):
            part = slice(start, start + size)
            pre_ref[:size, :] = dg(normed_ref[part, :], weight, 1, 0)
            for left, wide in spans(pre_ref.shape[1], 2 * PAIR):
                lanes = slice(left, left + wide)
                pre = pre_ref[:size, lanes]
                centered = pre - head_sum(pre, ones)
                inverse = lax.rsqrt(head_sum(centered * centered, ones) + EPS)
                hat = centered * inverse
                hat_ref[0, part, lanes] = hat
                inv_ref[0, part, lanes] = inverse
                low_ref[0, part, lanes] = ((hat * gain).astype(BF).astype(F32) * factor).astype(BF)

    @pl.when(section == 2)
    def _():
        for start, size in spans(token_ref.shape[0], CHUNK):
            part = slice(start, start + size)
            low_ref[0, part, :] = dg(normed_ref[part, :], weight, 1, 0).astype(BF)


def project(me, tokens, pieces):
    length, width = tokens.shape
    full = pl.BlockSpec((length, width), lambda s: (0, 0))
    wide = (GROUPS, *pieces[0].shape)
    return pl.pallas_call(
        project_kernel,
        grid=(3,),
        in_specs=[pl.BlockSpec(memory_space=pltpu.SMEM), full]
        + [pl.BlockSpec(memory_space=pl.ANY)] * GROUPS,
        out_specs=[
            pl.BlockSpec((1, length, width), lambda s: (s, 0, 0)),
            pl.BlockSpec((1, length, width), lambda s: (jnp.minimum(s, 1), 0, 0)),
            pl.BlockSpec((1, length, width), lambda s: (jnp.minimum(s, 1), 0, 0)),
            full,
            pl.BlockSpec(wide, lambda s: (0, 0, 0)),
        ],
        out_shape=[
            jax.ShapeDtypeStruct((3, length, width), BF),
            jax.ShapeDtypeStruct((2, length, width), F32),
            jax.ShapeDtypeStruct((2, length, width), F32),
            jax.ShapeDtypeStruct((length, width), BF),
            jax.ShapeDtypeStruct(wide, BF),
        ],
        scratch_shapes=[pltpu.VMEM((CHUNK, width), F32), pltpu.SemaphoreType.DMA((GROUPS,))],
        compiler_params=params(1),
        cost_estimate=cost(9 * length * width * width, 40 * length * width),
        name="project",
    )(me, tokens, *pieces)


def own_lanes(length, head):
    lane = lax.broadcasted_iota(jnp.int32, (length, PAIR), 1)
    return (lane // HEAD) == head


def attend_kernel(query_ref, key_ref, value_ref, near_ref, far_ref, exps_ref, mixed_ref, wide_ref, inv_ref):
    length = query_ref.shape[1]
    values = jnp.concatenate([value_ref[0], jnp.ones((length, PAIR), BF)], axis=1)
    for head in range(2):
        own = own_lanes(length, head)
        keys = jnp.where(own, key_ref[0], far_ref[...])
        for start, size in spans(length, CHUNK):
            part = slice(start, start + size)
            own_part = own_lanes(size, head)
            queries = jnp.where(own_part, query_ref[0, part, :], near_ref[part, :])
            exps = jnp.exp(dg(queries, keys, 1, 1)).astype(BF)
            exps_ref[head, part, :] = exps
            both = dg(exps, values, 1, 0)
            inverse = 1.0 / both[:, PAIR:]
            out = both[:, :PAIR] * inverse
            if head == 1:
                out = jnp.where(own_part, out, wide_ref[part, :])
                inverse = jnp.where(own_part, inverse, inv_ref[part, :])
                mixed_ref[part, :] = out.astype(BF)
            wide_ref[part, :] = out
            inv_ref[part, :] = inverse


def attend(low, near, far):
    _, length, width = low.shape
    pairs = width // PAIR
    lanes = pl.BlockSpec((length, PAIR), lambda p: (0, p))
    fixed = pl.BlockSpec((length, PAIR), lambda p: (0, 0))
    return pl.pallas_call(
        attend_kernel,
        grid=(pairs,),
        in_specs=[pl.BlockSpec((1, length, PAIR), lambda p, k=k: (k, 0, p)) for k in range(3)]
        + [fixed, fixed],
        out_specs=[pl.BlockSpec((2, length, length), lambda p: (p, 0, 0)), lanes, lanes, lanes],
        out_shape=[
            jax.ShapeDtypeStruct((2 * pairs, length, length), BF),
            jax.ShapeDtypeStruct((length, width), BF),
            jax.ShapeDtypeStruct((length, width), F32),
            jax.ShapeDtypeStruct((length, width), F32),
        ],
        compiler_params=params(1),
        cost_estimate=cost(pairs * 2 * 8 * PAIR * length * length, 24 * length * length),
        name="attend",
    )(low, low, low, near, far)


def mlp_kernel(
    normed_ref,
    cot_ref,
    mixed_ref,
    up_ref,
    down_ref,
    small_ref,
    branch_ref,
    back_ref,
    grads_ref,
    small_s,
    act_s,
    grad_s,
    up_s,
    down_s,
    sums_s,
    heads_s,
    owned_s,
    sems,
):
    step = pl.program_id(0)
    length, width = normed_ref.shape
    rows = width // GROUPS
    small_s[...] = small_rows(small_ref)
    bias = small_s[pl.ds(2 + step, 1), :]
    up = square(up_ref)
    down = square(down_ref)
    hidden = jnp.zeros((1, width), F32)
    for start, size in spans(length, CHUNK):
        part = slice(start, start + size)
        inner = dg(normed_ref[part, :], up, 1, 0) + bias
        cdf = 0.5 + 0.5 * lax.erf(inner * (0.5**0.5))
        pdf = jnp.exp(inner * inner * -0.5) * 0.3989422804014327
        act = (inner * cdf).astype(BF)
        grad = dg(cot_ref[part, :], down, 1, 1) * (cdf + inner * pdf)
        hidden = hidden + jnp.sum(grad, axis=0, keepdims=True)
        grad_low = grad.astype(BF)
        act_s[part, :] = act
        grad_s[part, :] = grad_low
        forward = dg(act, down, 1, 0)
        backward = dg(grad_low, up, 1, 1)

        @pl.when(step == 0)
        def _():
            branch_ref[part, :] = forward
            back_ref[part, :] = backward

        @pl.when(step > 0)
        def _():
            branch_ref[part, :] = branch_ref[part, :] + forward
            back_ref[part, :] = back_ref[part, :] + backward

    sums_s[pl.ds(1 + step, 1), :] = hidden
    groups = GROUPS // pl.num_programs(0)
    heads_copy = pltpu.make_async_copy(
        heads_s, grads_ref.at[:, pl.ds(8 * rows, rows), :], sems.at[2]
    )
    small_copy = pltpu.make_async_copy(
        owned_s, grads_ref.at[:, pl.ds(9 * rows, SMALL), :], sems.at[3]
    )

    @pl.when(step == 0)
    def _():
        heads_s[...] = dg(mixed_ref[...], cot_ref[...], 0, 0).astype(BF).reshape(heads_s.shape)
        heads_copy.start()
        total = jnp.zeros((1, width), F32)
        for start, size in spans(length, CHUNK):
            low = cot_ref[start : start + size, :].astype(F32)
            total = total + jnp.sum(low, axis=0, keepdims=True)
        sums_s[0:1, :] = total

    def copies(index):
        return (
            pltpu.make_async_copy(
                up_s, grads_ref.at[:, pl.ds(pl.multiple_of(index * rows, rows), rows), :], sems.at[0]
            ),
            pltpu.make_async_copy(
                down_s,
                grads_ref.at[pl.ds(index * groups, groups), pl.ds(4 * rows, 4 * rows), :],
                sems.at[1],
            ),
        )

    @pl.when(step > 0)
    def _():
        for copy in copies(step - 1):
            copy.wait()

    up_s[...] = dg(normed_ref[...], grad_s[...], 0, 0).astype(BF).reshape(up_s.shape)
    down_s[...] = dg(act_s[...], cot_ref[...], 0, 0).astype(BF).reshape(down_s.shape)
    for copy in copies(step):
        copy.start()

    @pl.when(step == pl.num_programs(0) - 1)
    def _():
        owner = lax.broadcasted_iota(jnp.int32, (GROUPS, 1, width), 0)
        lane = lax.broadcasted_iota(jnp.int32, (GROUPS, 1, width), 2)
        owned_s[...] = jnp.zeros_like(owned_s)
        kept = jnp.where(lane // rows == owner, sums_s[0:1, :][None], 0.0)
        parts = [kept]
        for k in range(4):
            mine = lane // (4 * rows) + k * (GROUPS // 4) == owner
            parts.append(jnp.where(mine, sums_s[k + 1 : k + 2, :][None], 0.0))
        for index, piece in enumerate(parts):
            owned_s[:, index : index + 1, :] = piece.astype(BF)
        small_copy.start()
        for copy in copies(step):
            copy.wait()
        heads_copy.wait()
        small_copy.wait()


def mlp(normed, cotangent, mixed, gathered, gathered_small):
    length, width = normed.shape
    rows = width // GROUPS
    steps = 4
    full = pl.BlockSpec((length, width), lambda s: (0, 0))
    return pl.pallas_call(
        mlp_kernel,
        grid=(steps,),
        in_specs=[
            full,
            full,
            full,
            pl.BlockSpec((GROUPS, rows, width), lambda s: (0, s, 0)),
            pl.BlockSpec((GROUPS // steps, steps * rows, width), lambda s: (s, 1, 0)),
            pl.BlockSpec((GROUPS, SMALL, width), lambda s: (0, 4 * rows // SMALL, 0)),
        ],
        out_specs=[
            full,
            full,
            pl.BlockSpec(memory_space=pl.ANY),
        ],
        out_shape=[
            jax.ShapeDtypeStruct((length, width), F32),
            jax.ShapeDtypeStruct((length, width), F32),
            jax.ShapeDtypeStruct((GROUPS, 9 * rows + SMALL, width), BF),
        ],
        scratch_shapes=[
            pltpu.VMEM((SMALL, width), F32),
            pltpu.VMEM((length, width), BF),
            pltpu.VMEM((length, width), BF),
            pltpu.VMEM((GROUPS, rows, width), BF),
            pltpu.VMEM((GROUPS // steps, steps * rows, width), BF),
            pltpu.VMEM((8, width), F32),
            pltpu.VMEM((GROUPS, rows, width), BF),
            pltpu.VMEM((GROUPS, SMALL, width), BF),
            pltpu.SemaphoreType.DMA((4,)),
        ],
        compiler_params=params(1),
        cost_estimate=cost(48 * length * width * width, 40 * length * width, 8 * length * width),
        name="mlp",
    )(normed, cotangent, mixed, gathered, gathered, gathered_small)


def backward_kernel(
    query_ref,
    key_ref,
    value_ref,
    exps_ref,
    wide_ref,
    inv_ref,
    cot_ref,
    heads_ref,
    small_ref,
    qhat_ref,
    khat_ref,
    qinv_ref,
    kinv_ref,
    grad_ref,
    sums_ref,
    heads_s,
    dot_s,
    delta_s,
    query_s,
    key_s,
    value_s,
):
    pair = pl.program_id(0)
    length = query_ref.shape[1]

    @pl.when(pair == 0)
    def _():
        heads_s[...] = square(heads_ref)
        sums_ref[...] = jnp.zeros_like(sums_ref)

    rows = small_rows(small_ref)
    flipped = block_ones(PAIR, 1.0, 1)
    head_rows = heads_s[pl.ds(pl.multiple_of(pair * PAIR, PAIR), PAIR), :]
    for start, size in spans(length, CHUNK):
        part = slice(start, start + size)
        grad = dg(cot_ref[part, :], head_rows, 1, 1) * inv_ref[part, :]
        low = grad.astype(BF)
        dot_s[part, :] = low
        delta_s[part, :] = head_sum(low.astype(F32) * wide_ref[part, :], flipped)

    for head in range(2):
        lane = lax.broadcasted_iota(jnp.int32, (length, PAIR), 1)
        own = (lane // HEAD) == head
        values = jnp.where(own, value_ref[0], jnp.where(lane % HEAD < 2, 1.0, 0.0).astype(BF))
        for start, size in spans(length, CHUNK):
            part = slice(start, start + size)
            lane_p = lax.broadcasted_iota(jnp.int32, (size, PAIR), 1)
            own_p = (lane_p // HEAD) == head
            high, rest = split_low(-delta_s[part, :])
            extra = jnp.where(
                lane_p % HEAD == 0, high, jnp.where(lane_p % HEAD == 1, rest, jnp.zeros_like(rest))
            )
            dots = dot_s[part, :]
            slopes = dg(jnp.where(own_p, dots, extra), values, 1, 1)
            exps = exps_ref[head, part, :]
            scores = (exps.astype(F32) * slopes).astype(BF)
            dq = dg(scores, key_ref[0], 1, 0)
            dk = dg(scores, query_ref[0, part, :], 0, 0)
            dv = dg(exps, dots, 0, 0)
            if head == 1:
                dq = jnp.where(own_p, dq, query_s[part, :])
            query_s[part, :] = dq
            if start == 0:
                key_s[head] = dk
                value_s[head] = dv
            else:
                key_s[head] = key_s[head] + dk
                value_s[head] = value_s[head] + dv

    ones = block_ones(PAIR, 1.0 / HEAD)
    for start, size in spans(length, CHUNK):
        part = slice(start, start + size)
        own_p = own_lanes(size, 0)
        both = (
            (query_s[part, :] * HEAD**-0.5, qhat_ref, qinv_ref, rows[6:7, :PAIR]),
            (
                jnp.where(own_p, key_s[0, part, :], key_s[1, part, :]),
                khat_ref,
                kinv_ref,
                rows[6:7, PAIR : 2 * PAIR],
            ),
        )
        for index, (grad, hat_ref, inverse_ref, gain) in enumerate(both):
            hat = hat_ref[0, part, :]
            product = grad * hat
            sums_ref[index : index + 1, :] += jnp.sum(product, axis=0, keepdims=True)
            mean = head_sum(grad * gain, ones)
            along = head_sum(product * gain, ones)
            grad_ref[index, part, :] = (
                inverse_ref[0, part, :] * (grad * gain - mean - hat * along)
            ).astype(BF)
        grad_ref[2, part, :] = jnp.where(own_p, value_s[0, part, :], value_s[1, part, :]).astype(BF)


def attend_back(low, exps, wide, inverse, cotangent, gathered, hat, inv):
    _, length, width = low.shape
    rows = width // GROUPS
    pairs = width // PAIR
    lanes = pl.BlockSpec((length, PAIR), lambda p: (0, p))

    def third(k):
        return pl.BlockSpec((1, length, PAIR), lambda p: (k, 0, p))

    return pl.pallas_call(
        backward_kernel,
        grid=(pairs,),
        in_specs=[third(k) for k in range(3)]
        + [
            pl.BlockSpec((2, length, length), lambda p: (p, 0, 0)),
            lanes,
            lanes,
            pl.BlockSpec((length, width), lambda p: (0, 0)),
            pl.BlockSpec((GROUPS, rows, width), lambda p: (0, 3, 0)),
            pl.BlockSpec((GROUPS, SMALL, width), lambda p: (0, 4 * rows // SMALL, 0)),
            third(0),
            third(1),
            third(0),
            third(1),
        ],
        out_specs=[
            pl.BlockSpec((3, length, PAIR), lambda p: (0, 0, p)),
            pl.BlockSpec((8, PAIR), lambda p: (0, 0)),
        ],
        out_shape=[
            jax.ShapeDtypeStruct((3, length, width), BF),
            jax.ShapeDtypeStruct((8, PAIR), F32),
        ],
        scratch_shapes=[
            pltpu.VMEM((width, width), BF),
            pltpu.VMEM((length, PAIR), BF),
            pltpu.VMEM((length, PAIR), F32),
            pltpu.VMEM((length, PAIR), F32),
            pltpu.VMEM((2, length, PAIR), F32),
            pltpu.VMEM((2, length, PAIR), F32),
        ],
        compiler_params=params(1),
        cost_estimate=cost(pairs * 2 * 16 * PAIR * length * length, 24 * length * length),
        name="attend_back",
    )(low, low, low, exps, wide, inverse, cotangent, gathered, gathered, hat, hat, inv, inv)


def weights_kernel(me_ref, normed_ref, grad_ref, sums_ref, send_ref, keep_ref, all_s):
    section = pl.program_id(0)
    width = normed_ref.shape[1]

    def hand_out(count):
        for slot in range(GROUPS // 2):
            other_y, ahead = 1 - slot // 4, slot % 4
            owner = source_of(me_ref[0], 0, other_y, 4 - ahead)
            partner = source_of(me_ref[0], 1, other_y, 4 - ahead)
            keep_ref[slot, :count, :] = all_s[owner, :count, :]
            send_ref[slot, :count, :] = all_s[partner, :count, :]

    @pl.when(section < 3)
    def _():
        all_s[...] = dg(normed_ref[...], grad_ref[0], 0, 0).astype(BF).reshape(all_s.shape)
        hand_out(all_s.shape[1])

    @pl.when(section == 3)
    def _():
        owner = lax.broadcasted_iota(jnp.int32, (GROUPS, 1, width), 0)
        lane = lax.broadcasted_iota(jnp.int32, (GROUPS, 1, width), 2)
        query = sums_ref[0:1, :HEAD] + sums_ref[0:1, HEAD:]
        key = sums_ref[1:2, :HEAD] + sums_ref[1:2, HEAD:]
        packed = jnp.concatenate([query, key, jnp.zeros((1, width - PAIR), F32)], axis=1)
        all_s[:, :SMALL, :] = jnp.zeros((GROUPS, SMALL, width), BF)
        mine = (lane % HEAD) // (HEAD // GROUPS) == owner
        all_s[:, 0:1, :] = jnp.where(mine, packed[None], 0.0).astype(BF)
        hand_out(SMALL)


def weight_grads(me, normed, grads, sums):
    _, length, width = grads.shape
    rows = width // GROUPS
    half = GROUPS // 2
    shape = jax.ShapeDtypeStruct((half, 3 * rows + SMALL, width), BF)
    spec = pl.BlockSpec((half, rows, width), lambda s: (0, s, 0))
    return pl.pallas_call(
        weights_kernel,
        grid=(4,),
        in_specs=[
            pl.BlockSpec(memory_space=pltpu.SMEM),
            pl.BlockSpec((length, width), lambda s: (0, 0)),
            pl.BlockSpec((1, length, width), lambda s: (jnp.minimum(s, 2), 0, 0)),
            pl.BlockSpec((8, PAIR), lambda s: (0, 0)),
        ],
        out_specs=[spec, spec],
        out_shape=[shape, shape],
        scratch_shapes=[pltpu.VMEM((GROUPS, rows, width), BF)],
        compiler_params=params(1),
        cost_estimate=cost(6 * length * width * width, 12 * length * width),
        name="weight_grads",
    )(me, normed, grads, sums)


def tail_kernel(
    grad_ref,
    weight_ref,
    small_ref,
    token_ref,
    cot_ref,
    mixed_ref,
    branch_ref,
    back_ref,
    out_ref,
    token_grad_ref,
    total_s,
):
    section = pl.program_id(0)
    length = token_ref.shape[0]
    weight = square(weight_ref)

    @pl.when(section == 0)
    def _():
        for start, size in spans(length, CHUNK):
            part = slice(start, start + size)
            total_s[part, :] = back_ref[part, :] + dg(grad_ref[0, part, :], weight, 1, 1)

    @pl.when((section > 0) & (section < 3))
    def _():
        for start, size in spans(length, CHUNK):
            part = slice(start, start + size)
            total_s[part, :] = total_s[part, :] + dg(grad_ref[0, part, :], weight, 1, 1)

    @pl.when(section == 3)
    def _():
        rows = small_rows(small_ref)
        for start, size in spans(length, CHUNK):
            part = slice(start, start + size)
            tokens = token_ref[part, :].astype(F32)
            attended = dg(mixed_ref[part, :], weight, 1, 0)
            out_ref[part, :] = (tokens + attended + branch_ref[part, :] + rows[1:2, :]).astype(BF)
            hat, inverse = row_norm(tokens)
            grad = total_s[part, :] * rows[0:1, :]
            mean = jnp.mean(grad, axis=-1, keepdims=True)
            along = jnp.mean(grad * hat, axis=-1, keepdims=True)
            token_grad_ref[part, :] = (
                cot_ref[part, :].astype(F32) + inverse * (grad - mean - hat * along)
            ).astype(BF)


def tail(grads, gathered, tokens, cotangent, mixed, branch, back):
    _, length, width = grads.shape
    rows = width // GROUPS
    full = pl.BlockSpec((length, width), lambda s: (0, 0))
    return pl.pallas_call(
        tail_kernel,
        grid=(4,),
        in_specs=[
            pl.BlockSpec((1, length, width), lambda s: (jnp.minimum(s, 2), 0, 0)),
            pl.BlockSpec((GROUPS, rows, width), lambda s: (0, s, 0)),
            pl.BlockSpec((GROUPS, SMALL, width), lambda s: (0, 4 * rows // SMALL, 0)),
            full,
            full,
            full,
            full,
            full,
        ],
        out_specs=[full, full],
        out_shape=[
            jax.ShapeDtypeStruct((length, width), BF),
            jax.ShapeDtypeStruct((length, width), BF),
        ],
        scratch_shapes=[pltpu.VMEM((length, width), F32)],
        compiler_params=params(1),
        cost_estimate=cost(8 * length * width * width, 24 * length * width),
        name="tail",
    )(grads, gathered, gathered, tokens, cotangent, mixed, branch, back)


def pack_kernel(me_ref, joined_ref, heads_ref, down_ref, norm_ref, out_ref, hid_ref, query_ref, key_ref, first_ref, second_ref):
    rows, width = heads_ref.shape
    me = me_ref[0]
    for k in range(3):
        first_ref[k * rows : (k + 1) * rows, :] = joined_ref[:, k * width : (k + 1) * width]
    first_ref[3 * rows : 4 * rows, :] = heads_ref[...]
    for k in range(4):
        second_ref[k * rows : (k + 1) * rows, :] = joined_ref[:, (3 + k) * width : (4 + k) * width]
    second_ref[4 * rows :, :] = down_ref[...]

    def spread(ref):
        size = ref.shape[1]
        line = lax.broadcasted_iota(jnp.int32, (size, width), 0)
        lane = lax.broadcasted_iota(jnp.int32, (size, width), 1)
        return dg(ref[...], jnp.where(lane % size == line, 1.0, 0.0).astype(BF), 1, 0)

    line = lax.broadcasted_iota(jnp.int32, (SMALL, width), 0)
    lane = lax.broadcasted_iota(jnp.int32, (SMALL, width), 1)
    thin, bias, head = norm_ref.shape[1], hid_ref.shape[1], query_ref.shape[1]
    per_row = width // bias
    mine = lane // thin == me
    head_mine = (lane % HEAD) // head == me
    small = jnp.where((line == 0) & mine, spread(norm_ref), 0.0)
    small = small + jnp.where((line == 1) & mine, spread(out_ref), 0.0)
    small = small + jnp.where(
        (line == 2 + me // per_row) & (lane // bias == me % per_row), spread(hid_ref), 0.0
    )
    small = small + jnp.where((line == 6) & head_mine & (lane < PAIR), spread(query_ref), 0.0)
    small = small + jnp.where(
        (line == 6) & head_mine & (lane >= PAIR) & (lane < 2 * PAIR), spread(key_ref), 0.0
    )
    first_ref[4 * rows :, :] = small.astype(BF)


def pack(me, joined, heads, down, *vectors):
    rows, width = heads.shape
    whole = pl.BlockSpec(memory_space=pltpu.VMEM)
    return pl.pallas_call(
        pack_kernel,
        in_specs=[pl.BlockSpec(memory_space=pltpu.SMEM)] + [whole] * 8,
        out_specs=[whole, whole],
        out_shape=[
            jax.ShapeDtypeStruct((4 * rows + SMALL, width), BF),
            jax.ShapeDtypeStruct((8 * rows, width), BF),
        ],
        compiler_params=pltpu.CompilerParams(vmem_limit_bytes=VMEM_LIMIT),
        name="pack",
    )(me, joined, heads, down, *(vector[None, :] for vector in vectors))


def place(vector, offset, total):
    return lax.dynamic_update_slice(jnp.zeros((total,), vector.dtype), vector, (offset,))


def device_of(z, y, core):
    return (z * 2 + y) * 2 + core


def route(core_flip, y_flip, z_ahead):
    return [
        (device_of(z, y, c), device_of((z + z_ahead) % 4, y ^ y_flip, c ^ core_flip))
        for z in range(4)
        for y in range(2)
        for c in range(2)
    ]


def send(array, core_flip, y_flip, z_ahead):
    return lax.ppermute(array, "fsdp", route(core_flip, y_flip, z_ahead))


def swap_rep(array):
    return lax.ppermute(array, "rep", [(0, 1), (1, 0)])


def gather_pieces(shard):
    line = [shard] + [send(shard, 0, 0, k) for k in (1, 2, 3)]
    plane = line + [send(piece, 0, 1, 0) for piece in line]
    return plane + [send(piece, 1, 0, 0) for piece in plane]


def add_low(left, right):
    return left.astype(F32) + right.astype(F32)


def reduce_pieces(outgoing, kept):
    half = GROUPS // 4
    came = send(outgoing, 1, 0, 0)
    came_y = send(add_low(kept[:half], came[:half]).astype(BF), 0, 1, 0)
    plane = (add_low(kept[half:], came[half:]) + came_y.astype(F32)).astype(BF)
    total = plane[0].astype(F32)
    for k in (1, 2, 3):
        total = total + send(plane[k], 0, 0, k).astype(F32)
    return total.astype(BF)


def stack_columns(shard, first, count, width):
    return [shard[:, (first + k) * width : (first + k + 1) * width] for k in range(count)]


def regroup(gathered, section_rows):
    devices, _, width = gathered.shape
    if devices == GROUPS:
        return gathered
    fold = devices // GROUPS
    parts, start = [], 0
    for rows, small in section_rows:
        piece = gathered[:, start : start + rows, :]
        start += rows
        if small:
            parts.append(piece.reshape(GROUPS, fold, rows, width).sum(1))
        else:
            parts.append(piece.reshape(GROUPS, fold * rows, width))
    return jnp.concatenate(parts, axis=1)


def ungroup(grouped, section_rows, devices):
    if devices == GROUPS:
        return grouped
    fold = devices // GROUPS
    width = grouped.shape[2]
    parts, start = [], 0
    for rows, small in section_rows:
        wide = rows if small else rows * fold
        piece = grouped[:, start : start + wide, :]
        start += wide
        if small:
            parts.append(jnp.repeat(piece, fold, axis=0))
        else:
            parts.append(piece.reshape(devices, rows, width))
    return jnp.concatenate(parts, axis=1)


def per_device(
    devices,
    tokens_in,
    token_image,
    joined_weight,
    heads_weight,
    down_weight,
    norm_gain,
    query_gain,
    key_gain,
    hidden_bias,
    output_bias,
    cotangent,
):
    length, width = tokens_in.shape
    rows = joined_weight.shape[0]
    me = lax.axis_index("fsdp")
    thin, bias_thin, head_thin = norm_gain.shape[0], hidden_bias.shape[0], query_gain.shape[0]
    chained = devices == GROUPS
    first_rows = [(rows, False)] * 4 + [(SMALL, True)]
    second_rows = [(rows, False)] * 4 + [(4 * rows, False)]
    early_rows = second_rows + first_rows[3:]
    late_rows = first_rows[1:]

    if chained:
        place_in = me.astype(jnp.int32)[None]
        first, second = pack(
            place_in,
            joined_weight,
            heads_weight,
            down_weight,
            norm_gain,
            output_bias,
            hidden_bias,
            query_gain,
            key_gain,
        )
        pieces = gather_pieces(first)
    else:
        place_in = jnp.zeros((1,), jnp.int32)
        small = (
            place(norm_gain, me * thin, SMALL * width)
            + place(output_bias, width + me * thin, SMALL * width)
            + place(hidden_bias, 2 * width + me * bias_thin, SMALL * width)
        )
        for index, vector in enumerate((query_gain, query_gain, key_gain, key_gain)):
            small = small + place(vector, 6 * width + index * HEAD + me * head_thin, SMALL * width)
        first = jnp.concatenate(
            stack_columns(joined_weight, 0, 3, width)
            + [heads_weight, small.reshape(SMALL, width)],
            axis=0,
        )
        second = jnp.concatenate(stack_columns(joined_weight, 3, 4, width) + [down_weight], axis=0)
        natural = regroup(lax.all_gather(first, "fsdp", axis=0), first_rows)
        pieces = [natural[source_of(0, *path)] for path in ROUTES]
    gathered_mlp = regroup(lax.all_gather(second, "fsdp", axis=0), second_rows)

    lane = lax.broadcasted_iota(jnp.int32, (length, PAIR), 1) % HEAD
    same = lane == token_image[:, None]
    near = jnp.where(same, 1.0, 0.0).astype(BF)
    far = jnp.where(same | (lane >= 6), 0.0, FAR).astype(BF)

    low, hat, inv, normed, gathered = project(place_in, tokens_in, pieces)
    exps, mixed, wide, inverse = attend(low, near, far)
    branch, back, early = mlp(normed, cotangent, mixed, gathered_mlp, gathered)
    early_shard = lax.psum_scatter(
        ungroup(early, early_rows, devices), "fsdp", scatter_dimension=0, tiled=True
    )[0]

    inverse, _ = lax.optimization_barrier((inverse, branch))
    grads, sums = attend_back(low, exps, wide, inverse, cotangent, gathered, hat, inv)
    outgoing, kept = weight_grads(place_in, normed, grads, sums)
    if chained:
        late_shard = reduce_pieces(outgoing, kept)
    else:
        natural = jnp.stack([outgoing, kept]).reshape(2, 2, 4, *kept.shape[1:])[::-1, ::-1]
        natural = natural.transpose(2, 1, 0, 3, 4).reshape(GROUPS, *kept.shape[1:])
        late_shard = lax.psum_scatter(
            ungroup(natural, late_rows, devices), "fsdp", scatter_dimension=0, tiled=True
        )[0]
    block_out, grad_tokens = tail(grads, gathered, tokens_in, cotangent, mixed, branch, back)

    late_total = add_low(late_shard, swap_rep(late_shard))
    early_total = add_low(early_shard, swap_rep(early_shard))

    total_joined = jnp.concatenate(
        [late_total[k * rows : (k + 1) * rows] for k in range(3)]
        + [early_total[k * rows : (k + 1) * rows] for k in range(4)],
        axis=1,
    )
    total_heads = early_total[8 * rows : 9 * rows]
    total_down = early_total[4 * rows : 8 * rows]
    total_norm = jnp.sum(joined_weight.astype(F32) * total_joined, axis=1) / norm_gain.astype(F32)

    def take(table, row, offset, size):
        return lax.dynamic_slice(table, (row, offset), (1, size))[0]

    flat = me * bias_thin
    early_small, late_small = early_total[9 * rows :], late_total[3 * rows :]
    total_output = take(early_small, 0, me * thin, thin)
    total_hidden = take(early_small, 1 + flat // width, flat % width, bias_thin)
    total_query = take(late_small, 0, me * head_thin, head_thin)
    total_key = take(late_small, 0, HEAD + me * head_thin, head_thin)
    return (
        block_out,
        grad_tokens,
        total_joined,
        total_heads,
        total_down,
        total_norm,
        total_query,
        total_key,
        total_hidden,
        total_output,
    )


def solution(mesh):
    tokens, shard, thin = P(("rep", "fsdp"), None), P("fsdp", None), P("fsdp")
    return jax.shard_map(
        functools.partial(per_device, mesh.shape["fsdp"]),
        mesh=mesh,
        in_specs=(tokens, P(("rep", "fsdp")), shard, shard, shard, thin, thin, thin, thin, thin, tokens),
        out_specs=(tokens, tokens, shard, shard, shard, thin, thin, thin, thin, thin),
        check_vma=False,
    )
```

```python
import functools

import jax
import jax.numpy as jnp
from jax import lax
from jax.experimental import pallas as pl
from jax.experimental.pallas import tpu as pltpu
from jax.sharding import PartitionSpec as P

F32 = jnp.float32
BF = jnp.bfloat16
EPS = 1e-06
GROUPS = 16
SMALL = 16
HEAD = 64
PAIR = 128
CHUNK = 256
FAR = -512.0
VMEM_LIMIT = 62 << 20


def dg(left, right, left_dim, right_dim):
    return lax.dot_general(
        left, right, (((left_dim,), (right_dim,)), ((), ())), preferred_element_type=F32
    )


def spans(total, step):
    return [(start, min(step, total - start)) for start in range(0, total, step)]


def split_low(values):
    high = values.astype(BF)
    return high, (values - high.astype(F32)).astype(BF)


def block_ones(size, scale, flip=0):
    row = lax.broadcasted_iota(jnp.int32, (size, size), 0) // HEAD
    col = lax.broadcasted_iota(jnp.int32, (size, size), 1) // HEAD
    return jnp.where(row == (col ^ flip), scale, 0.0).astype(BF)


def head_sum(values, ones):
    high, low = split_low(values)
    return dg(high, ones, 1, 0) + dg(low, ones, 1, 0)


def row_norm(rows):
    mean = jnp.mean(rows, axis=-1, keepdims=True)
    centered = rows - mean
    variance = jnp.mean(centered * centered, axis=-1, keepdims=True)
    inverse = lax.rsqrt(variance + EPS)
    return centered * inverse, inverse


def square(block_ref):
    groups, rows, width = block_ref.shape
    return block_ref[...].reshape(groups * rows, width)


def params(steps):
    return pltpu.CompilerParams(
        dimension_semantics=("arbitrary",) * steps, vmem_limit_bytes=VMEM_LIMIT
    )


def cost(flops, moved, special=0):
    return pl.CostEstimate(flops=int(flops), bytes_accessed=int(moved), transcendentals=int(special))


def source_of(me, core_flip, y_flip, z_back):
    z, y, core = me // 4, (me // 2) % 2, me % 2
    z, y, core = (z + 4 - z_back) % 4, (y + y_flip) % 2, (core + core_flip) % 2
    return (z * 2 + y) * 2 + core


ROUTES = [(c, y, k) for c in range(2) for y in range(2) for k in range(4)]


def project_kernel(normed_ref, weight_ref, rows_ref, low_ref, hat_ref, inv_ref, pre_ref):
    section = pl.program_id(0)
    length = normed_ref.shape[0]
    weight = square(weight_ref)

    @pl.when(section < 2)
    def _():
        ones = block_ones(2 * PAIR, 1.0 / HEAD)
        gain_pair = jnp.where(section == 0, rows_ref[6:7, :PAIR], rows_ref[6:7, PAIR : 2 * PAIR])
        gain = jnp.concatenate([gain_pair, gain_pair], axis=1)
        factor = jnp.where(section == 0, HEAD**-0.5, 1.0).astype(F32)
        for start, size in spans(length, CHUNK):
            part = slice(start, start + size)
            pre_ref[:size, :] = dg(normed_ref[part, :], weight, 1, 0)
            for left, wide in spans(pre_ref.shape[1], 2 * PAIR):
                lanes = slice(left, left + wide)
                pre = pre_ref[:size, lanes]
                centered = pre - head_sum(pre, ones)
                inverse = lax.rsqrt(head_sum(centered * centered, ones) + EPS)
                hat = centered * inverse
                hat_ref[0, part, lanes] = hat
                inv_ref[0, part, lanes] = inverse
                low_ref[0, part, lanes] = ((hat * gain).astype(BF).astype(F32) * factor).astype(BF)

    @pl.when(section == 2)
    def _():
        for start, size in spans(length, CHUNK):
            part = slice(start, start + size)
            low_ref[0, part, :] = dg(normed_ref[part, :], weight, 1, 0).astype(BF)


def project(normed, gathered, rows):
    length, width = normed.shape
    group = width // GROUPS
    return pl.pallas_call(
        project_kernel,
        grid=(3,),
        in_specs=[
            pl.BlockSpec((length, width), lambda s: (0, 0)),
            pl.BlockSpec((GROUPS, group, width), lambda s: (0, s, 0)),
            pl.BlockSpec((SMALL, width), lambda s: (0, 0)),
        ],
        out_specs=[
            pl.BlockSpec((1, length, width), lambda s: (s, 0, 0)),
            pl.BlockSpec((1, length, width), lambda s: (jnp.minimum(s, 1), 0, 0)),
            pl.BlockSpec((1, length, width), lambda s: (jnp.minimum(s, 1), 0, 0)),
        ],
        out_shape=[
            jax.ShapeDtypeStruct((3, length, width), BF),
            jax.ShapeDtypeStruct((2, length, width), F32),
            jax.ShapeDtypeStruct((2, length, width), F32),
        ],
        scratch_shapes=[pltpu.VMEM((CHUNK, width), F32)],
        compiler_params=params(1),
        cost_estimate=cost(9 * length * width * width, 36 * length * width),
        name="project",
    )(normed, gathered, rows)


def own_lanes(length, head):
    lane = lax.broadcasted_iota(jnp.int32, (length, PAIR), 1)
    return (lane // HEAD) == head


def attend_kernel(query_ref, key_ref, value_ref, near_ref, far_ref, exps_ref, mixed_ref, wide_ref, inv_ref):
    length = query_ref.shape[1]
    values = jnp.concatenate([value_ref[0], jnp.ones((length, PAIR), BF)], axis=1)
    for head in range(2):
        own = own_lanes(length, head)
        keys = jnp.where(own, key_ref[0], far_ref[...])
        for start, size in spans(length, CHUNK):
            part = slice(start, start + size)
            own_part = own_lanes(size, head)
            queries = jnp.where(own_part, query_ref[0, part, :], near_ref[part, :])
            exps = jnp.exp(dg(queries, keys, 1, 1)).astype(BF)
            exps_ref[head, part, :] = exps
            both = dg(exps, values, 1, 0)
            inverse = 1.0 / both[:, PAIR:]
            out = both[:, :PAIR] * inverse
            if head == 1:
                out = jnp.where(own_part, out, wide_ref[part, :])
                inverse = jnp.where(own_part, inverse, inv_ref[part, :])
                mixed_ref[part, :] = out.astype(BF)
            wide_ref[part, :] = out
            inv_ref[part, :] = inverse


def attend(low, near, far):
    _, length, width = low.shape
    pairs = width // PAIR
    lanes = pl.BlockSpec((length, PAIR), lambda p: (0, p))
    fixed = pl.BlockSpec((length, PAIR), lambda p: (0, 0))
    return pl.pallas_call(
        attend_kernel,
        grid=(pairs,),
        in_specs=[pl.BlockSpec((1, length, PAIR), lambda p, k=k: (k, 0, p)) for k in range(3)]
        + [fixed, fixed],
        out_specs=[pl.BlockSpec((2, length, length), lambda p: (p, 0, 0)), lanes, lanes, lanes],
        out_shape=[
            jax.ShapeDtypeStruct((2 * pairs, length, length), BF),
            jax.ShapeDtypeStruct((length, width), BF),
            jax.ShapeDtypeStruct((length, width), F32),
            jax.ShapeDtypeStruct((length, width), F32),
        ],
        compiler_params=params(1),
        cost_estimate=cost(pairs * 2 * 8 * PAIR * length * length, 24 * length * length),
        name="attend",
    )(low, low, low, near, far)


def source_of(me, core_flip, y_flip, z_back):
    z, y, core = me // 4, (me // 2) % 2, me % 2
    z, y, core = (z + 4 - z_back) % 4, (y + y_flip) % 2, (core + core_flip) % 2
    return (z * 2 + y) * 2 + core


ROUTES = [(c, y, k) for c in range(2) for y in range(2) for k in range(4)]


def mlp_kernel(me_ref, token_ref, cot_ref, up_ref, *refs):
    pieces = refs[:GROUPS]
    normed_ref, rows_ref, all_ref, act_ref, back_ref, grads_ref = refs[GROUPS : GROUPS + 6]
    up_s, down_s, sums_s, owned_s, sems, piece_sems = refs[GROUPS + 6 :]
    step = pl.program_id(0)
    length, width = token_ref.shape
    group = width // GROUPS
    steps = GROUPS // 4

    @pl.when(step == 0)
    def _():
        arrivals = [
            pltpu.make_async_copy(
                piece, all_ref.at[source_of(me_ref[0], *path)], piece_sems.at[index]
            )
            for index, (piece, path) in enumerate(zip(pieces, ROUTES))
        ]
        for copy in arrivals:
            copy.start()
        total = jnp.zeros((1, width), F32)
        for start, size in spans(length, CHUNK):
            low = cot_ref[start : start + size, :].astype(F32)
            total = total + jnp.sum(low, axis=0, keepdims=True)
        sums_s[0:1, :] = total
        for copy in arrivals:
            copy.wait()
        rows_ref[...] = jnp.sum(all_ref[:, 4 * group :, :].astype(F32), axis=0)
        for start, size in spans(length, CHUNK):
            hat, _ = row_norm(token_ref[start : start + size, :].astype(F32))
            normed_ref[start : start + size, :] = (hat * rows_ref[0:1, :]).astype(BF)

    bias = rows_ref[pl.ds(2 + step, 1), :]
    up = square(up_ref)
    down = all_ref[pl.ds(step * steps, steps), : 4 * group, :].reshape(width, width)
    hidden = jnp.zeros((1, width), F32)
    for start, size in spans(length, CHUNK):
        part = slice(start, start + size)
        inner = dg(normed_ref[part, :], up, 1, 0) + bias
        cdf = 0.5 + 0.5 * lax.erf(inner * (0.5**0.5))
        pdf = jnp.exp(inner * inner * -0.5) * 0.3989422804014327
        act_ref[0, part, :] = (inner * cdf).astype(BF)
        grad = dg(cot_ref[part, :], down, 1, 1) * (cdf + inner * pdf)
        hidden = hidden + jnp.sum(grad, axis=0, keepdims=True)
        back_ref[0, part, :] = grad.astype(BF)
    sums_s[pl.ds(1 + step, 1), :] = hidden
    small_copy = pltpu.make_async_copy(
        owned_s, grads_ref.at[:, pl.ds(8 * group, SMALL), :], sems.at[2]
    )

    def copies(index):
        return (
            pltpu.make_async_copy(
                up_s,
                grads_ref.at[:, pl.ds(pl.multiple_of(index * group, group), group), :],
                sems.at[0],
            ),
            pltpu.make_async_copy(
                down_s,
                grads_ref.at[pl.ds(index * steps, steps), pl.ds(4 * group, 4 * group), :],
                sems.at[1],
            ),
        )

    @pl.when(step > 0)
    def _():
        for copy in copies(step - 1):
            copy.wait()

    up_s[...] = dg(normed_ref[...], back_ref[0], 0, 0).astype(BF).reshape(up_s.shape)
    down_s[...] = dg(act_ref[0], cot_ref[...], 0, 0).astype(BF).reshape(down_s.shape)
    for copy in copies(step):
        copy.start()

    @pl.when(step == pl.num_programs(0) - 1)
    def _():
        owner = lax.broadcasted_iota(jnp.int32, (GROUPS, 1, width), 0)
        lane = lax.broadcasted_iota(jnp.int32, (GROUPS, 1, width), 2)
        owned_s[...] = jnp.zeros_like(owned_s)
        parts = [jnp.where(lane // group == owner, sums_s[0:1, :][None], 0.0)]
        for k in range(4):
            mine = lane // (4 * group) + k * steps == owner
            parts.append(jnp.where(mine, sums_s[k + 1 : k + 2, :][None], 0.0))
        for index, piece in enumerate(parts):
            owned_s[:, index : index + 1, :] = piece.astype(BF)
        small_copy.start()
        for copy in copies(step):
            copy.wait()
        small_copy.wait()


def mlp(me, tokens, cotangent, gathered_up, pieces):
    length, width = tokens.shape
    group = width // GROUPS
    steps = 4
    full = pl.BlockSpec((length, width), lambda s: (0, 0))
    wide = (GROUPS, *pieces[0].shape)
    block = pl.BlockSpec((1, length, width), lambda s: (s, 0, 0))
    return pl.pallas_call(
        mlp_kernel,
        grid=(steps,),
        in_specs=[
            pl.BlockSpec(memory_space=pltpu.SMEM),
            full,
            full,
            pl.BlockSpec((GROUPS, group, width), lambda s: (0, s, 0)),
        ]
        + [pl.BlockSpec(memory_space=pl.ANY)] * GROUPS,
        out_specs=[
            full,
            pl.BlockSpec((SMALL, width), lambda s: (0, 0)),
            pl.BlockSpec(wide, lambda s: (0, 0, 0)),
            block,
            block,
            pl.BlockSpec(memory_space=pl.ANY),
        ],
        out_shape=[
            jax.ShapeDtypeStruct((length, width), BF),
            jax.ShapeDtypeStruct((SMALL, width), F32),
            jax.ShapeDtypeStruct(wide, BF),
            jax.ShapeDtypeStruct((steps, length, width), BF),
            jax.ShapeDtypeStruct((steps, length, width), BF),
            jax.ShapeDtypeStruct((GROUPS, 8 * group + SMALL, width), BF),
        ],
        scratch_shapes=[
            pltpu.VMEM((GROUPS, group, width), BF),
            pltpu.VMEM((GROUPS // steps, steps * group, width), BF),
            pltpu.VMEM((8, width), F32),
            pltpu.VMEM((GROUPS, SMALL, width), BF),
            pltpu.SemaphoreType.DMA((3,)),
            pltpu.SemaphoreType.DMA((GROUPS,)),
        ],
        compiler_params=params(1),
        cost_estimate=cost(32 * length * width * width, 32 * length * width, 8 * length * width),
        name="mlp",
    )(me, tokens, cotangent, gathered_up, *pieces)


def backward_kernel(
    query_ref,
    key_ref,
    value_ref,
    exps_ref,
    wide_ref,
    inv_ref,
    cot_ref,
    heads_ref,
    rows_ref,
    qhat_ref,
    khat_ref,
    qinv_ref,
    kinv_ref,
    grad_ref,
    sums_ref,
    heads_s,
    dot_s,
    delta_s,
    query_s,
    key_s,
    value_s,
):
    pair = pl.program_id(0)
    length = query_ref.shape[1]

    @pl.when(pair == 0)
    def _():
        heads_s[...] = square(heads_ref)
        sums_ref[...] = jnp.zeros_like(sums_ref)

    rows = rows_ref[...]
    flipped = block_ones(PAIR, 1.0, 1)
    head_rows = heads_s[pl.ds(pl.multiple_of(pair * PAIR, PAIR), PAIR), :]
    for start, size in spans(length, CHUNK):
        part = slice(start, start + size)
        grad = dg(cot_ref[part, :], head_rows, 1, 1) * inv_ref[part, :]
        low = grad.astype(BF)
        dot_s[part, :] = low
        delta_s[part, :] = head_sum(low.astype(F32) * wide_ref[part, :], flipped)

    for head in range(2):
        lane = lax.broadcasted_iota(jnp.int32, (length, PAIR), 1)
        own = (lane // HEAD) == head
        values = jnp.where(own, value_ref[0], jnp.where(lane % HEAD < 2, 1.0, 0.0).astype(BF))
        for start, size in spans(length, CHUNK):
            part = slice(start, start + size)
            lane_p = lax.broadcasted_iota(jnp.int32, (size, PAIR), 1)
            own_p = (lane_p // HEAD) == head
            high, rest = split_low(-delta_s[part, :])
            extra = jnp.where(
                lane_p % HEAD == 0, high, jnp.where(lane_p % HEAD == 1, rest, jnp.zeros_like(rest))
            )
            dots = dot_s[part, :]
            slopes = dg(jnp.where(own_p, dots, extra), values, 1, 1)
            exps = exps_ref[head, part, :]
            scores = (exps.astype(F32) * slopes).astype(BF)
            dq = dg(scores, key_ref[0], 1, 0)
            dk = dg(scores, query_ref[0, part, :], 0, 0)
            dv = dg(exps, dots, 0, 0)
            if head == 1:
                dq = jnp.where(own_p, dq, query_s[part, :])
            query_s[part, :] = dq
            if start == 0:
                key_s[head] = dk
                value_s[head] = dv
            else:
                key_s[head] = key_s[head] + dk
                value_s[head] = value_s[head] + dv

    ones = block_ones(PAIR, 1.0 / HEAD)
    for start, size in spans(length, CHUNK):
        part = slice(start, start + size)
        own_p = own_lanes(size, 0)
        both = (
            (query_s[part, :] * HEAD**-0.5, qhat_ref, qinv_ref, rows[6:7, :PAIR]),
            (
                jnp.where(own_p, key_s[0, part, :], key_s[1, part, :]),
                khat_ref,
                kinv_ref,
                rows[6:7, PAIR : 2 * PAIR],
            ),
        )
        for index, (grad, hat_ref, inverse_ref, gain) in enumerate(both):
            hat = hat_ref[0, part, :]
            product = grad * hat
            sums_ref[index : index + 1, :] += jnp.sum(product, axis=0, keepdims=True)
            mean = head_sum(grad * gain, ones)
            along = head_sum(product * gain, ones)
            grad_ref[index, part, :] = (
                inverse_ref[0, part, :] * (grad * gain - mean - hat * along)
            ).astype(BF)
        grad_ref[2, part, :] = jnp.where(own_p, value_s[0, part, :], value_s[1, part, :]).astype(BF)


def attend_back(low, exps, wide, inverse, cotangent, gathered, small, hat, inv):
    _, length, width = low.shape
    rows = width // GROUPS
    pairs = width // PAIR
    lanes = pl.BlockSpec((length, PAIR), lambda p: (0, p))

    def third(k):
        return pl.BlockSpec((1, length, PAIR), lambda p: (k, 0, p))

    return pl.pallas_call(
        backward_kernel,
        grid=(pairs,),
        in_specs=[third(k) for k in range(3)]
        + [
            pl.BlockSpec((2, length, length), lambda p: (p, 0, 0)),
            lanes,
            lanes,
            pl.BlockSpec((length, width), lambda p: (0, 0)),
            pl.BlockSpec((GROUPS, rows, width), lambda p: (0, 3, 0)),
            pl.BlockSpec((SMALL, width), lambda p: (0, 0)),
            third(0),
            third(1),
            third(0),
            third(1),
        ],
        out_specs=[
            pl.BlockSpec((3, length, PAIR), lambda p: (0, 0, p)),
            pl.BlockSpec((8, PAIR), lambda p: (0, 0)),
        ],
        out_shape=[
            jax.ShapeDtypeStruct((3, length, width), BF),
            jax.ShapeDtypeStruct((8, PAIR), F32),
        ],
        scratch_shapes=[
            pltpu.VMEM((width, width), BF),
            pltpu.VMEM((length, PAIR), BF),
            pltpu.VMEM((length, PAIR), F32),
            pltpu.VMEM((length, PAIR), F32),
            pltpu.VMEM((2, length, PAIR), F32),
            pltpu.VMEM((2, length, PAIR), F32),
        ],
        compiler_params=params(1),
        cost_estimate=cost(pairs * 2 * 16 * PAIR * length * length, 24 * length * length),
        name="attend_back",
    )(low, low, low, exps, wide, inverse, cotangent, gathered, small, hat, hat, inv, inv)


def weights_kernel(me_ref, normed_ref, grad_ref, sums_ref, send_ref, keep_ref, all_s):
    section = pl.program_id(0)
    width = normed_ref.shape[1]

    def hand_out(count):
        for slot in range(GROUPS // 2):
            other_y, ahead = 1 - slot // 4, slot % 4
            owner = source_of(me_ref[0], 0, other_y, 4 - ahead)
            partner = source_of(me_ref[0], 1, other_y, 4 - ahead)
            keep_ref[slot, :count, :] = all_s[owner, :count, :]
            send_ref[slot, :count, :] = all_s[partner, :count, :]

    @pl.when(section < 3)
    def _():
        all_s[...] = dg(normed_ref[...], grad_ref[0], 0, 0).astype(BF).reshape(all_s.shape)
        hand_out(all_s.shape[1])

    @pl.when(section == 3)
    def _():
        owner = lax.broadcasted_iota(jnp.int32, (GROUPS, 1, width), 0)
        lane = lax.broadcasted_iota(jnp.int32, (GROUPS, 1, width), 2)
        query = sums_ref[0:1, :HEAD] + sums_ref[0:1, HEAD:]
        key = sums_ref[1:2, :HEAD] + sums_ref[1:2, HEAD:]
        packed = jnp.concatenate([query, key, jnp.zeros((1, width - PAIR), F32)], axis=1)
        all_s[:, :SMALL, :] = jnp.zeros((GROUPS, SMALL, width), BF)
        mine = (lane % HEAD) // (HEAD // GROUPS) == owner
        all_s[:, 0:1, :] = jnp.where(mine, packed[None], 0.0).astype(BF)
        hand_out(SMALL)


def weight_grads(me, normed, grads, sums):
    _, length, width = grads.shape
    rows = width // GROUPS
    half = GROUPS // 2
    shape = jax.ShapeDtypeStruct((half, 3 * rows + SMALL, width), BF)
    spec = pl.BlockSpec((half, rows, width), lambda s: (0, s, 0))
    return pl.pallas_call(
        weights_kernel,
        grid=(4,),
        in_specs=[
            pl.BlockSpec(memory_space=pltpu.SMEM),
            pl.BlockSpec((length, width), lambda s: (0, 0)),
            pl.BlockSpec((1, length, width), lambda s: (jnp.minimum(s, 2), 0, 0)),
            pl.BlockSpec((8, PAIR), lambda s: (0, 0)),
        ],
        out_specs=[spec, spec],
        out_shape=[shape, shape],
        scratch_shapes=[pltpu.VMEM((GROUPS, rows, width), BF)],
        compiler_params=params(1),
        cost_estimate=cost(6 * length * width * width, 12 * length * width),
        name="weight_grads",
    )(me, normed, grads, sums)


def token_kernel(late_ref, early_ref, late_w_ref, early_w_ref, rows_ref, token_ref, cot_ref, out_ref, total_s):
    section = pl.program_id(0)
    length = token_ref.shape[0]

    def accumulate(grad_ref, weight_ref, first):
        weight = square(weight_ref)
        for start, size in spans(length, CHUNK):
            part = slice(start, start + size)
            term = dg(grad_ref[0, part, :], weight, 1, 1)
            total_s[part, :] = term if first else total_s[part, :] + term

    @pl.when(section == 0)
    def _():
        accumulate(early_ref, early_w_ref, True)

    @pl.when((section > 0) & (section < 4))
    def _():
        accumulate(early_ref, early_w_ref, False)

    @pl.when(section >= 4)
    def _():
        accumulate(late_ref, late_w_ref, False)

    @pl.when(section == pl.num_programs(0) - 1)
    def _():
        for start, size in spans(length, CHUNK):
            part = slice(start, start + size)
            hat, inverse = row_norm(token_ref[part, :].astype(F32))
            grad = total_s[part, :] * rows_ref[0:1, :]
            mean = jnp.mean(grad, axis=-1, keepdims=True)
            along = jnp.mean(grad * hat, axis=-1, keepdims=True)
            out_ref[part, :] = (
                cot_ref[part, :].astype(F32) + inverse * (grad - mean - hat * along)
            ).astype(BF)


def token_grads(late, early, gathered, gathered_up, rows, tokens, cotangent):
    _, length, width = late.shape
    group = width // GROUPS
    full = pl.BlockSpec((length, width), lambda s: (0, 0))

    def early_at(s):
        return jnp.minimum(s, 3)

    def late_at(s):
        return jnp.maximum(s - 4, 0)

    return pl.pallas_call(
        token_kernel,
        grid=(7,),
        in_specs=[
            pl.BlockSpec((1, length, width), lambda s: (late_at(s), 0, 0)),
            pl.BlockSpec((1, length, width), lambda s: (early_at(s), 0, 0)),
            pl.BlockSpec((GROUPS, group, width), lambda s: (0, late_at(s), 0)),
            pl.BlockSpec((GROUPS, group, width), lambda s: (0, early_at(s), 0)),
            pl.BlockSpec((SMALL, width), lambda s: (0, 0)),
            full,
            full,
        ],
        out_specs=full,
        out_shape=jax.ShapeDtypeStruct((length, width), BF),
        scratch_shapes=[pltpu.VMEM((length, width), F32)],
        compiler_params=params(1),
        cost_estimate=cost(14 * length * width * width, 24 * length * width),
        name="token_grads",
    )(late, early, gathered, gathered_up, rows, tokens, cotangent)


def output_kernel(act_ref, down_ref, heads_ref, mixed_ref, rows_ref, token_ref, out_ref, total_s):
    step = pl.program_id(0)
    length, width = token_ref.shape
    down = square(down_ref)

    @pl.when(step == 0)
    def _():
        heads = square(heads_ref)
        for start, size in spans(length, CHUNK):
            part = slice(start, start + size)
            total_s[part, :] = (
                token_ref[part, :].astype(F32)
                + rows_ref[1:2, :]
                + dg(mixed_ref[part, :], heads, 1, 0)
            )

    for start, size in spans(length, CHUNK):
        part = slice(start, start + size)
        total_s[part, :] = total_s[part, :] + dg(act_ref[0, part, :], down, 1, 0)

    @pl.when(step == pl.num_programs(0) - 1)
    def _():
        out_ref[...] = total_s[...].astype(BF)


def block_output(act, gathered_down, gathered, mixed, rows, tokens):
    steps, length, width = act.shape
    group = width // GROUPS
    full = pl.BlockSpec((length, width), lambda s: (0, 0))
    return pl.pallas_call(
        output_kernel,
        grid=(steps,),
        in_specs=[
            pl.BlockSpec((1, length, width), lambda s: (s, 0, 0)),
            pl.BlockSpec((GROUPS // steps, 4 * group, width), lambda s: (s, 0, 0)),
            pl.BlockSpec((GROUPS, group, width), lambda s: (0, 3, 0)),
            full,
            pl.BlockSpec((SMALL, width), lambda s: (0, 0)),
            full,
        ],
        out_specs=full,
        out_shape=jax.ShapeDtypeStruct((length, width), BF),
        scratch_shapes=[pltpu.VMEM((length, width), F32)],
        compiler_params=params(1),
        cost_estimate=cost(10 * length * width * width, 20 * length * width),
        name="block_output",
    )(act, gathered_down, gathered, mixed, rows, tokens)


def pack_kernel(me_ref, joined_ref, heads_ref, down_ref, norm_ref, out_ref, hid_ref, query_ref, key_ref, first_ref, second_ref, third_ref):
    rows, width = heads_ref.shape
    me = me_ref[0]
    first_ref[: 4 * rows, :] = down_ref[...]
    for k in range(4):
        second_ref[k * rows : (k + 1) * rows, :] = joined_ref[:, (3 + k) * width : (4 + k) * width]
    for k in range(3):
        third_ref[k * rows : (k + 1) * rows, :] = joined_ref[:, k * width : (k + 1) * width]
    third_ref[3 * rows :, :] = heads_ref[...]

    def spread(ref):
        size = ref.shape[1]
        line = lax.broadcasted_iota(jnp.int32, (size, width), 0)
        lane = lax.broadcasted_iota(jnp.int32, (size, width), 1)
        return dg(ref[...], jnp.where(lane % size == line, 1.0, 0.0).astype(BF), 1, 0)

    line = lax.broadcasted_iota(jnp.int32, (SMALL, width), 0)
    lane = lax.broadcasted_iota(jnp.int32, (SMALL, width), 1)
    thin, bias, head = norm_ref.shape[1], hid_ref.shape[1], query_ref.shape[1]
    per_row = width // bias
    mine = lane // thin == me
    head_mine = (lane % HEAD) // head == me
    small = jnp.where((line == 0) & mine, spread(norm_ref), 0.0)
    small = small + jnp.where((line == 1) & mine, spread(out_ref), 0.0)
    small = small + jnp.where(
        (line == 2 + me // per_row) & (lane // bias == me % per_row), spread(hid_ref), 0.0
    )
    small = small + jnp.where((line == 6) & head_mine & (lane < PAIR), spread(query_ref), 0.0)
    small = small + jnp.where(
        (line == 6) & head_mine & (lane >= PAIR) & (lane < 2 * PAIR), spread(key_ref), 0.0
    )
    first_ref[4 * rows :, :] = small.astype(BF)


def pack(me, joined, heads, down, *vectors):
    rows, width = heads.shape
    whole = pl.BlockSpec(memory_space=pltpu.VMEM)
    return pl.pallas_call(
        pack_kernel,
        in_specs=[pl.BlockSpec(memory_space=pltpu.SMEM)] + [whole] * 8,
        out_specs=[whole, whole, whole],
        out_shape=[
            jax.ShapeDtypeStruct((4 * rows + SMALL, width), BF),
            jax.ShapeDtypeStruct((4 * rows, width), BF),
            jax.ShapeDtypeStruct((4 * rows, width), BF),
        ],
        compiler_params=pltpu.CompilerParams(vmem_limit_bytes=VMEM_LIMIT),
        name="pack",
    )(me, joined, heads, down, *(vector[None, :] for vector in vectors))


def place(vector, offset, total):
    return lax.dynamic_update_slice(jnp.zeros((total,), vector.dtype), vector, (offset,))


def device_of(z, y, core):
    return (z * 2 + y) * 2 + core


def route(core_flip, y_flip, z_ahead):
    return [
        (device_of(z, y, c), device_of((z + z_ahead) % 4, y ^ y_flip, c ^ core_flip))
        for z in range(4)
        for y in range(2)
        for c in range(2)
    ]


def send(array, core_flip, y_flip, z_ahead):
    return lax.ppermute(array, "fsdp", route(core_flip, y_flip, z_ahead))


def swap_rep(array):
    return lax.ppermute(array, "rep", [(0, 1), (1, 0)])


def gather_pieces(shard):
    line = [shard] + [send(shard, 0, 0, k) for k in (1, 2, 3)]
    plane = line + [send(piece, 0, 1, 0) for piece in line]
    return plane + [send(piece, 1, 0, 0) for piece in plane]


def add_low(left, right):
    return left.astype(F32) + right.astype(F32)


def after(value, filler):
    return lax.optimization_barrier((value, filler))[0]


def reduce_pieces(outgoing, kept, under_y, under_z):
    half = GROUPS // 4
    came = send(outgoing, 1, 0, 0)
    came_y = after(send(add_low(kept[:half], came[:half]).astype(BF), 0, 1, 0), under_y)
    plane = (add_low(kept[half:], came[half:]) + came_y.astype(F32)).astype(BF)
    total = plane[0].astype(F32)
    for k in (1, 2, 3):
        total = total + after(send(plane[k], 0, 0, k), under_z).astype(F32)
    return total.astype(BF)


def stack_columns(shard, first, count, width):
    return [shard[:, (first + k) * width : (first + k + 1) * width] for k in range(count)]


def regroup(gathered, section_rows):
    devices, _, width = gathered.shape
    if devices == GROUPS:
        return gathered
    fold = devices // GROUPS
    parts, start = [], 0
    for rows, small in section_rows:
        piece = gathered[:, start : start + rows, :]
        start += rows
        if small:
            parts.append(piece.reshape(GROUPS, fold, rows, width).sum(1))
        else:
            parts.append(piece.reshape(GROUPS, fold * rows, width))
    return jnp.concatenate(parts, axis=1)


def ungroup(grouped, section_rows, devices):
    if devices == GROUPS:
        return grouped
    fold = devices // GROUPS
    width = grouped.shape[2]
    parts, start = [], 0
    for rows, small in section_rows:
        wide = rows if small else rows * fold
        piece = grouped[:, start : start + wide, :]
        start += wide
        if small:
            parts.append(jnp.repeat(piece, fold, axis=0))
        else:
            parts.append(piece.reshape(devices, rows, width))
    return jnp.concatenate(parts, axis=1)


def per_device(
    devices,
    tokens_in,
    token_image,
    joined_weight,
    heads_weight,
    down_weight,
    norm_gain,
    query_gain,
    key_gain,
    hidden_bias,
    output_bias,
    cotangent,
):
    length, width = tokens_in.shape
    rows = joined_weight.shape[0]
    me = lax.axis_index("fsdp")
    thin, bias_thin, head_thin = norm_gain.shape[0], hidden_bias.shape[0], query_gain.shape[0]
    chained = devices == GROUPS
    fourths = [(rows, False)] * 4
    first_rows = [(4 * rows, False), (SMALL, True)]
    early_rows = fourths + first_rows
    late_rows = fourths[:3] + first_rows[1:]

    def scatter(array, section_rows):
        array = ungroup(array, section_rows, devices)
        return lax.psum_scatter(array, "fsdp", scatter_dimension=0, tiled=True)[0]

    if chained:
        place_in = me.astype(jnp.int32)[None]
        first, second, third = pack(
            place_in,
            joined_weight,
            heads_weight,
            down_weight,
            norm_gain,
            output_bias,
            hidden_bias,
            query_gain,
            key_gain,
        )
        pieces = gather_pieces(first)
    else:
        place_in = jnp.zeros((1,), jnp.int32)
        small = (
            place(norm_gain, me * thin, SMALL * width)
            + place(output_bias, width + me * thin, SMALL * width)
            + place(hidden_bias, 2 * width + me * bias_thin, SMALL * width)
        )
        for index, vector in enumerate((query_gain, query_gain, key_gain, key_gain)):
            small = small + place(vector, 6 * width + index * HEAD + me * head_thin, SMALL * width)
        first = jnp.concatenate([down_weight, small.reshape(SMALL, width)], axis=0)
        second = jnp.concatenate(stack_columns(joined_weight, 3, 4, width), axis=0)
        third = jnp.concatenate(
            stack_columns(joined_weight, 0, 3, width) + [heads_weight], axis=0
        )
        natural = regroup(lax.all_gather(first, "fsdp", axis=0), first_rows)
        pieces = [natural[source_of(0, *path)] for path in ROUTES]
    gathered_up = regroup(lax.all_gather(second, "fsdp", axis=0), fourths)
    third = after(third, pieces[-1])
    gathered = regroup(lax.all_gather(third, "fsdp", axis=0), fourths)

    lane = lax.broadcasted_iota(jnp.int32, (length, PAIR), 1) % HEAD
    same = lane == token_image[:, None]
    near = jnp.where(same, 1.0, 0.0).astype(BF)
    far = jnp.where(same | (lane >= 6), 0.0, FAR).astype(BF)

    normed, small_table, gathered_down, act, inner_grads, early = mlp(
        place_in, tokens_in, cotangent, gathered_up, pieces
    )
    early_shard = scatter(early, early_rows)
    low, hat, inv = project(normed, gathered, small_table)
    exps, mixed, wide, inverse = attend(low, near, far)
    heads_grad = dg(mixed, cotangent, 0, 0).astype(BF).reshape(GROUPS, width // GROUPS, width)
    heads_shard = scatter(heads_grad, fourths[:1])
    inverse = after(inverse, heads_grad)
    grads, sums = attend_back(low, exps, wide, inverse, cotangent, gathered, small_table, hat, inv)
    outgoing, kept = weight_grads(place_in, normed, grads, sums)
    grad_tokens = token_grads(
        grads, inner_grads, gathered, gathered_up, small_table, tokens_in, cotangent
    )
    held, _ = lax.optimization_barrier((mixed, grad_tokens))
    block_out = block_output(act, gathered_down, gathered, held, small_table, tokens_in)
    if chained:
        late_shard = reduce_pieces(outgoing, kept, grad_tokens, block_out)
    else:
        natural = jnp.stack([outgoing, kept]).reshape(2, 2, 4, *kept.shape[1:])[::-1, ::-1]
        natural = natural.transpose(2, 1, 0, 3, 4).reshape(GROUPS, *kept.shape[1:])
        late_shard = scatter(natural, late_rows)

    early_total = add_low(early_shard, swap_rep(early_shard))
    heads_total = add_low(heads_shard, swap_rep(heads_shard))
    late_total = add_low(late_shard, swap_rep(late_shard))

    total_joined = jnp.concatenate(
        [late_total[k * rows : (k + 1) * rows] for k in range(3)]
        + [early_total[k * rows : (k + 1) * rows] for k in range(4)],
        axis=1,
    )
    total_heads = heads_total
    total_down = early_total[4 * rows : 8 * rows]
    total_norm = jnp.sum(joined_weight.astype(F32) * total_joined, axis=1) / norm_gain.astype(F32)

    def take(table, row, offset, size):
        return lax.dynamic_slice(table, (row, offset), (1, size))[0]

    flat = me * bias_thin
    early_small, late_small = early_total[8 * rows :], late_total[3 * rows :]
    total_output = take(early_small, 0, me * thin, thin)
    total_hidden = take(early_small, 1 + flat // width, flat % width, bias_thin)
    total_query = take(late_small, 0, me * head_thin, head_thin)
    total_key = take(late_small, 0, HEAD + me * head_thin, head_thin)
    return (
        block_out,
        grad_tokens,
        total_joined,
        total_heads,
        total_down,
        total_norm,
        total_query,
        total_key,
        total_hidden,
        total_output,
    )


def solution(mesh):
    tokens, shard, thin = P(("rep", "fsdp"), None), P("fsdp", None), P("fsdp")
    return jax.shard_map(
        functools.partial(per_device, mesh.shape["fsdp"]),
        mesh=mesh,
        in_specs=(tokens, P(("rep", "fsdp")), shard, shard, shard, thin, thin, thin, thin, thin, tokens),
        out_specs=(tokens, tokens, shard, shard, shard, thin, thin, thin, thin, thin),
        check_vma=False,
    )
```
